32 devices in a mesh: ens: 2 (over y), lon: 4 (over z), dom: 4 (over x, core).
Axes of the slice: x: 2, y: 2, z: 4, core: 2. Of those that a mesh axis runs over, the one named last changes fastest.
Arguments:
- particles: bfloat16 [16, 69, 96, 256], P(('ens', 'dom'), None, 'lon'), parts along dimension 0, may hold values from -6 to 6
- observed: bfloat16 [138, 96, 256], P('ens', 'lon'), parts along dimension 0, may hold values from -6 to 6
- precision: float32 [192, 256], P(('ens', 'lon')), parts along dimension 0, may hold values from 0.25 to 12, as said below
- stations: int32 [192, 256], P(('ens', 'lon')), parts along dimension 0, may hold values 0 or 1
- ancestors: int32 [16], P(('ens', 'dom')), parts along dimension 0, may hold values from 0 to 7
- tempering: float32 [2], P('ens'), parts along dimension 0, may hold values from 1 to 4
- w_in: bfloat16 [3, 3, 64, 69], replicated, may hold values from -0.25 to 0.25
- w_mid: bfloat16 [3, 3, 64, 64], replicated, may hold values from -0.25 to 0.25
- w_out: bfloat16 [3, 3, 69, 64], replicated, may hold values from -0.25 to 0.25
Outputs:
- new_particles: bfloat16 [16, 69, 96, 256], P(('ens', 'dom'), None, 'lon'), parts along dimension 0
- weights: float32 [16], P(('ens', 'dom')), parts along dimension 0
The draws below stay inside these ranges and needn't reach their ends.
There are 2 independent parts, one for each index of `ens`. The reference program is written for one: setup_inputs(seed, part) draws one part's arguments, and reference() takes and returns one part's arrays. A program takes and returns all parts, laid end to end along the dimension named above; an argument that names none is the same for every part. Nothing has to cross between parts.
Inputs may be any that keep to these rules, and one draw needn't show every extreme that they name: `precision`: positive everywhere; no other structure is promised. Slot s continues particle ancestors[s]; a particle may be continued by several slots or by none.
All inputs are finite; a program needn't handle non-finite values. No bound on the sum of `stations` on one device may be relied on, other than what follows from the above.
Results may differ from the reference program's by a relative error of at most 0.0021.
Values may be sent and summed in bfloat16 or wider, within the bound.
A program may use at most 128 MiB of HBM per device.

```python
import math
import jax
import jax.numpy as jnp
import numpy as np
from jax import lax

VARS = 69
HID = 64
LAT = 256
P_SIZE = 8
LON = 96


def draw_precision(key, part):
    column = jnp.arange(LON, dtype=jnp.float32)
    east_ramp = 1.0 + 2.0 * column / max(LON - 1, 1)
    rough_part = jnp.exp(jax.random.uniform(key, (LON, LAT), jnp.float32, jnp.log(0.5), jnp.log(2.0)))
    return (rough_part * east_ramp[:, None]).astype(jnp.float32)


def plant(array, own_key, low, high):
    place = [jax.random.randint(jax.random.fold_in(own_key, axis), (), 0, length) for axis, length in enumerate(array.shape)]
    longest = array.shape.index(max(array.shape))
    next_to = place[:longest] + [(place[longest] + 1) % array.shape[longest]] + place[longest + 1:]
    return array.at[tuple(place)].set(low).at[tuple(next_to)].set(high)


def block_scale(stream_key, extent, shards, smallest, top_value):
    def one(position, blocks):
        heights = jax.random.uniform(jax.random.fold_in(jax.random.fold_in(stream_key, 6), position), (blocks,), jnp.float32, smallest / len(shards), top_value / len(shards))
        return jnp.repeat(jnp.exp(heights), extent[position] // blocks).reshape((-1,) + (1,) * (len(extent) - position - 1))

    factor_of = one(*shards[0])
    for cut in shards[1:]:
        factor_of = factor_of * one(*cut)
    return factor_of


def rank_table(amount, skew):
    weights = [(1 << 20) // math.isqrt(grade ** skew) + 1 for grade in range(1, amount + 1)]
    scale = 1 + sum(weights) // (1 << 30)
    return np.cumsum(np.array([max(1, weight // scale) for weight in weights]))


def ranked(stream_key, extent, count, skew):
    table = rank_table(count, skew)
    lot = jax.random.randint(jax.random.fold_in(stream_key, 1), extent, 0, int(table[count - 1]))
    standing = jnp.searchsorted(jnp.asarray(table, jnp.int32), lot, side="right")
    return jax.random.permutation(jax.random.fold_in(stream_key, 2), count)[standing].astype(jnp.int32)


def centred(own_key, extent, width, bound, pieces=(), held_as=jnp.bfloat16):
    factor_of = block_scale(own_key, extent, pieces, -0.22, 0.18) if pieces else 1.0
    drawn = jax.random.normal(own_key, extent, jnp.float32) * width * factor_of
    return jnp.minimum(jnp.maximum(drawn, -bound), bound).astype(held_as)


def setup_inputs(seed: int = 0, part: int = 0) -> dict:
    arg_keys = jax.random.split(jax.random.key(seed), 10)
    own_keys = jax.random.split(jax.random.fold_in(arg_keys[9], part), 10)
    return {
        "particles": centred(own_keys[0], (P_SIZE, VARS, LON, LAT), 1.0, 6.0, ((0, 4), (2, 4))),
        "observed": centred(own_keys[1], (VARS, LON, LAT), 1.0, 6.0, ((1, 4),)),
        "precision": draw_precision(jax.random.fold_in(jax.random.fold_in(arg_keys[9], part), 71), part),
        "stations": plant((jax.random.randint(own_keys[3], (LON, LAT), 0, 3) < 1).astype(jnp.int32), jax.random.fold_in(own_keys[3], 1), 0, 1),
        "ancestors": plant(ranked(own_keys[4], (P_SIZE,), P_SIZE, 2), jax.random.fold_in(own_keys[4], 3), 0, P_SIZE - 1).astype(jnp.int32),
        "tempering": jnp.clip(jnp.exp(jax.random.uniform(own_keys[5], (1,), jnp.float32, math.log(1.0), math.log(4.0))), 1.0, 4.0),
        "w_in": centred(arg_keys[6], (3, 3, HID, VARS), (9 * VARS) ** -0.5, 0.25),
        "w_mid": centred(arg_keys[7], (3, 3, HID, HID), (9 * HID) ** -0.5, 0.25),
        "w_out": centred(arg_keys[8], (3, 3, VARS, HID), (9 * HID) ** -0.5, 0.25),
    }


def conv_wrap(field, weight):
    lon_cols = field.shape[1]
    lat_rows = field.shape[2]
    extended = jnp.concatenate([field[:, -1:, :], field, field[:, :1, :]], axis=1)
    extended = jnp.pad(extended, ((0, 0), (0, 0), (1, 1)))
    summed = jnp.zeros((weight.shape[2], lon_cols, lat_rows), jnp.float32)
    for row_tap in range(3):
        for col_tap in range(3):
            window = extended[:, row_tap:row_tap + lon_cols, col_tap:col_tap + lat_rows].astype(jnp.float32)
            summed = summed + jnp.einsum('oc,cxy->oxy', weight[row_tap, col_tap].astype(jnp.float32), window)
    return summed

def denoise_one(states, observed, obs_weight, w_in, w_mid, w_out):
    first_act = jax.nn.silu(conv_wrap(states, w_in)).astype(jnp.bfloat16)
    second_act = jax.nn.silu(conv_wrap(first_act, w_mid)).astype(jnp.bfloat16)
    noise_pred = conv_wrap(second_act, w_out)
    current = states.astype(jnp.float32)
    updated = current - 0.5 * noise_pred + 0.25 * obs_weight[None] * (observed.astype(jnp.float32) - current)
    return updated.astype(jnp.bfloat16)

def reference(particles, observed, precision, stations, ancestors, tempering, w_in, w_mid, w_out):
    obs_weight = stations.astype(jnp.float32) * precision
    observed_f = observed.astype(jnp.float32)

    def misfit_one(states):
        misfit_cell = states.astype(jnp.float32) - observed_f
        return jnp.sum(obs_weight[None] * misfit_cell * misfit_cell)
    misfit = lax.map(misfit_one, particles)
    center = jnp.mean(misfit)
    deviation = misfit - center
    spread = jnp.sqrt(jnp.mean(deviation * deviation) + 1.0)
    log_weights = -0.5 * tempering[0] * deviation / spread
    expo = jnp.exp(log_weights)
    weights = expo / jnp.sum(expo)
    updated = lax.map(lambda states: denoise_one(states, observed, obs_weight, w_in, w_mid, w_out), particles)
    new_particles = jnp.take(updated, ancestors.astype(jnp.int32), axis=0)
    return (new_particles, weights)
```

```python
import functools

import jax
import jax.numpy as jnp
from jax import lax
from jax.experimental import pallas as pl
from jax.experimental.pallas import tpu as pltpu
from jax.sharding import PartitionSpec as P


def pad_to(count, step):
    return -(-count // step) * step


def stacked_taps(weight, out_rows, in_rows):
    _, _, outs, ins = weight.shape
    w = jnp.pad(weight, ((0, 0), (0, 0), (0, out_rows - outs), (0, in_rows - ins)))
    return w.transpose(1, 2, 0, 3).reshape(3 * out_rows, 3 * in_rows)


def conv_column(src_ref, w, x, in_rows, out_rows, first, last):
    window = src_ref[x * in_rows : (x + 3) * in_rows, :]
    p = jnp.dot(w, window, preferred_element_type=jnp.float32)
    lat = p.shape[1]
    below = pltpu.roll(p[:out_rows], 1, 1)
    above = pltpu.roll(p[2 * out_rows :], lat - 1, 1)
    return (
        p[out_rows : 2 * out_rows]
        + jnp.where(first, 0.0, below)
        + jnp.where(last, 0.0, above)
    )


def silu(v):
    half = 0.5 * v
    return half + half * jnp.tanh(half)


def step_kernel(spans, cin, hid, edges, *refs):
    if edges:
        low_ref, high_ref, *refs = refs
    mid_ref, obs_ref, ow_ref, w1_ref, w2_ref, w3_ref, out_ref, ext, a1, a2 = refs
    cols, nvars, lat = mid_ref.shape[1:]
    lane_h = lax.broadcasted_iota(jnp.int32, (hid, lat), 1)
    lane_o = lax.broadcasted_iota(jnp.int32, (cin, lat), 1)
    first_h, last_h = lane_h == 0, lane_h == lat - 1
    first_o, last_o = lane_o == 0, lane_o == lat - 1

    @pl.when(pl.program_id(0) == 0)
    def _():
        ext[...] = jnp.zeros_like(ext)

    at = 0
    for s, (lo, hi) in enumerate(spans):
        for k, x in enumerate(range(lo - 3, hi + 3)):
            if x < 0:
                column = low_ref[0, x + 3]
            elif x >= cols:
                column = high_ref[0, x - cols]
            else:
                column = mid_ref[0, x]
            ext[s, k * cin : k * cin + nvars, :] = column
        for x in range(hi - lo + 4):
            v = conv_column(ext.at[s], w1_ref[...], x, cin, hid, first_h, last_h)
            a1[s, x * hid : (x + 1) * hid, :] = silu(v).astype(jnp.bfloat16)
        for x in range(hi - lo + 2):
            v = conv_column(a1.at[s], w2_ref[...], x, hid, hid, first_h, last_h)
            a2[s, x * hid : (x + 1) * hid, :] = silu(v).astype(jnp.bfloat16)
        for x in range(hi - lo):
            noise = conv_column(a2.at[s], w3_ref[...], x, hid, cin, first_o, last_o)[:nvars]
            current = ext[s, (x + 3) * cin : (x + 4) * cin, :].astype(jnp.float32)[:nvars]
            seen = obs_ref[lo + x].astype(jnp.float32)
            gain = 0.25 * ow_ref[lo + x]
            new = current - 0.5 * noise + gain * (seen - current)
            out_ref[0, at] = new.astype(jnp.bfloat16)
            at += 1


def update_chunk(spans, edges, mid, observed, obs_weight, w1, w2, w3, cin, hid):
    slots, _, nvars, lat = mid.shape
    step = sum(hi - lo for lo, hi in spans)
    widest = max(hi - lo for lo, hi in spans)
    whole = lambda a: pl.BlockSpec(a.shape, lambda p: (0,) * a.ndim)
    own = lambda a: pl.BlockSpec((1,) + a.shape[1:], lambda p: (p, 0, 0, 0))
    return pl.pallas_call(
        functools.partial(step_kernel, spans, cin, hid, bool(edges)),
        out_shape=jax.ShapeDtypeStruct((slots, step, nvars, lat), jnp.bfloat16),
        grid=(slots,),
        in_specs=[own(a) for a in (*edges, mid)]
        + [whole(a) for a in (observed, obs_weight, w1, w2, w3)],
        out_specs=pl.BlockSpec((1, step, nvars, lat), lambda p: (p, 0, 0, 0)),
        scratch_shapes=[
            pltpu.VMEM((len(spans), (widest + 6) * cin, lat), jnp.bfloat16),
            pltpu.VMEM((len(spans), (widest + 4) * hid, lat), jnp.bfloat16),
            pltpu.VMEM((len(spans), (widest + 2) * hid, lat), jnp.bfloat16),
        ],
        compiler_params=pltpu.CompilerParams(vmem_limit_bytes=56 << 20),
        cost_estimate=pl.CostEstimate(flops=0, bytes_accessed=1024, transcendentals=0),
        name="update_chunk",
    )(*edges, mid, observed, obs_weight, w1, w2, w3)


def exchange_kernel(n_lon, mid_ref, sums_ref, low_ref, high_ref, total_ref, parts, edge_send, edge_recv, lon_send, lon_recv):
    lon = lax.axis_index("lon")
    cols = mid_ref.shape[1]

    def lon_at(k):
        return {"lon": lax.rem(lon + k, n_lon)}

    barrier = pltpu.get_barrier_semaphore()
    for k in range(1, n_lon):
        pl.semaphore_signal(barrier, inc=1, device_id=lon_at(k), device_id_type=pl.DeviceIdType.MESH)
    pl.semaphore_wait(barrier, n_lon - 1)

    def send(src, dst, s, r, target):
        copy = pltpu.make_async_remote_copy(
            src_ref=src, dst_ref=dst, send_sem=s, recv_sem=r,
            device_id=target, device_id_type=pl.DeviceIdType.MESH,
        )
        copy.start()
        return copy

    edges = [
        send(mid_ref.at[:, cols - 3 : cols], low_ref, edge_send.at[0], edge_recv.at[0], lon_at(1)),
        send(mid_ref.at[:, 0:3], high_ref, edge_send.at[1], edge_recv.at[1], lon_at(n_lon - 1)),
    ]
    parts[lon] = sums_ref[...]
    over_lon = [
        send(sums_ref, parts.at[lon], lon_send.at[k - 1], lon_recv.at[k - 1], lon_at(k))
        for k in range(1, n_lon)
    ]
    for copy in over_lon:
        copy.wait()
    band_sum = parts[0]
    for k in range(1, n_lon):
        band_sum = band_sum + parts[k]
    total_ref[...] = band_sum
    for copy in edges:
        copy.wait()


def exchange(mid, sums, n_lon):
    slots, _, nvars, lat = mid.shape
    edge = jax.ShapeDtypeStruct((slots, 3, nvars, lat), mid.dtype)
    vmem = pl.BlockSpec(memory_space=pltpu.VMEM)
    return pl.pallas_call(
        functools.partial(exchange_kernel, n_lon),
        out_shape=(edge, edge, jax.ShapeDtypeStruct(sums.shape, jnp.float32)),
        in_specs=[pl.BlockSpec(memory_space=pl.ANY), vmem],
        out_specs=(vmem, vmem, vmem),
        scratch_shapes=[
            pltpu.VMEM((n_lon,) + sums.shape, jnp.float32),
            pltpu.SemaphoreType.DMA((2,)),
            pltpu.SemaphoreType.DMA((2,)),
            pltpu.SemaphoreType.DMA((n_lon - 1,)),
            pltpu.SemaphoreType.DMA((n_lon - 1,)),
        ],
        compiler_params=pltpu.CompilerParams(collective_id=0, has_side_effects=True),
        cost_estimate=pl.CostEstimate(flops=0, bytes_accessed=1024, transcendentals=0),
        name="exchange",
    )(mid, sums)


def across(u):
    n = lax.axis_size("dom")
    return [u] + [
        lax.ppermute(u, "dom", [(d, (d + 2 * k) % n) for d in range(n)]) for k in range(1, n // 2)
    ]


def pick_kernel(slots, base, codes_ref, *refs):
    *pieces, out_ref = refs
    if base == 0:
        received_ref, *pieces = pieces
    for s in range(slots):
        for m in range(len(pieces) * slots):
            wanted = codes_ref[base + s] == m
            if base == 0:
                wanted = wanted & (codes_ref[2 * slots + s] == 1)

            @pl.when(wanted)
            def _():
                out_ref[s] = pieces[m // slots][m % slots]

        if base == 0:

            @pl.when(codes_ref[2 * slots + s] == 0)
            def _():
                out_ref[s] = received_ref[s]


def pick(codes, base, arrays):
    u = arrays[0]
    slots = u.shape[0]
    vmem = pl.BlockSpec(memory_space=pltpu.VMEM)
    return pl.pallas_call(
        functools.partial(pick_kernel, slots, base),
        out_shape=jax.ShapeDtypeStruct(u.shape, u.dtype),
        in_specs=[pl.BlockSpec(memory_space=pltpu.SMEM)] + [vmem] * len(arrays),
        out_specs=vmem,
        compiler_params=pltpu.CompilerParams(vmem_limit_bytes=24 << 20),
        cost_estimate=pl.CostEstimate(flops=0, bytes_accessed=1024, transcendentals=0),
        name="pick",
    )(codes, *arrays)


def weight_kernel(slots, t_ref, *refs):
    *part_refs, out_ref = refs
    shape = out_ref.shape
    real = lax.broadcasted_iota(jnp.int32, shape, 0) < slots
    count = len(part_refs) * slots

    def over_particles(rows):
        total = rows[0]
        for row in rows[1:]:
            total = total + row
        return jnp.sum(total, axis=0, keepdims=True)

    misfits = [jnp.broadcast_to(jnp.sum(r[...], axis=1, keepdims=True), shape) for r in part_refs]
    center = over_particles([jnp.where(real, m, 0.0) for m in misfits]) / count
    deviations = [jnp.where(real, m - center, 0.0) for m in misfits]
    spread = jnp.sqrt(over_particles([d * d for d in deviations]) / count + 1.0)
    expos = [jnp.where(real, jnp.exp(-0.5 * t_ref[0] * d / spread), 0.0) for d in deviations]
    out_ref[...] = expos[0] / over_particles(expos)


def own_weights_of(parts, tempering, slots):
    vmem = pl.BlockSpec(memory_space=pltpu.VMEM)
    out = pl.pallas_call(
        functools.partial(weight_kernel, slots),
        out_shape=jax.ShapeDtypeStruct(parts[0].shape, jnp.float32),
        in_specs=[pl.BlockSpec(memory_space=pltpu.SMEM)] + [vmem] * len(parts),
        out_specs=vmem,
        name="own_weights",
    )(tempering, *parts)
    return out[:slots, 0]


def many_chips(particles, observed, precision, stations, ancestors, tempering, w_in, w_mid, w_out):
    slots, nvars, cols, lat = particles.shape
    hid = w_mid.shape[2]
    cin = pad_to(nvars, 16)
    n_dom, n_lon = lax.axis_size("dom"), lax.axis_size("lon")
    me = lax.axis_index("dom")
    mid = particles.transpose(0, 2, 1, 3)
    sibling_anc = lax.ppermute(ancestors, "dom", [(d, d ^ 1) for d in range(n_dom)])

    obs_weight = stations.astype(jnp.float32) * precision
    wanted = jnp.concatenate([ancestors, sibling_anc])
    owner = lax.div(wanted, slots)
    chips = n_dom // 2
    steps = lax.rem(lax.shift_right_logical(me, 1) - lax.div(owner, 2) + chips, chips)
    candidate = steps * slots + lax.rem(wanted, slots)
    here = lax.rem(owner, 2) == (me & 1)

    obs_columns = observed.transpose(1, 0, 2)
    ow_columns = obs_weight[:, None, :]
    w1 = stacked_taps(w_in, hid, cin)
    w2 = stacked_taps(w_mid, hid, hid)
    w3 = stacked_taps(w_out, cin, hid)

    update = lambda spans, edges: update_chunk(
        spans, edges, mid, obs_columns, ow_columns, w1, w2, w3, cin, hid
    )
    u = update([(3, cols - 3)], [])
    groups = [across(u)]

    late_weight, _ = lax.optimization_barrier((obs_weight, u))
    misfit_cell = particles.astype(jnp.float32) - observed.astype(jnp.float32)[None]
    local_sums = jnp.sum(late_weight[None, None] * misfit_cell * misfit_cell, axis=(1, 2))
    sums = jnp.sum(local_sums.reshape(slots, lat // 128, 128), axis=1)
    sums = jnp.pad(sums, ((0, pad_to(slots, 8) - slots), (0, 0)))
    low, high, band_sums = exchange(mid, sums, n_lon)
    groups.append(across(update([(0, 3), (cols - 3, cols)], [low, high])))

    parts = [band_sums] + [
        lax.ppermute(band_sums, "dom", [(d, (d + k) % n_dom) for d in range(n_dom)])
        for k in range(1, n_dom)
    ]
    own_weights = own_weights_of(parts, tempering, slots)

    codes = jnp.concatenate([candidate, here[:slots].astype(jnp.int32)])
    groups = lax.optimization_barrier(groups)
    results = []
    for pieces in groups:
        sent = pick(codes, slots, pieces)
        received = lax.ppermute(sent, "dom", [(d, d ^ 1) for d in range(n_dom)])
        results.append(pick(codes, 0, [received, *pieces]))
    inner, sides = results
    new_columns = jnp.concatenate([sides[:, :3], inner, sides[:, 3:]], axis=1)
    return (new_columns.transpose(0, 2, 1, 3), own_weights)


MESH = pl.DeviceIdType.MESH
FIXED = 2


def column_chunks(cols):
    inner = list(range(3, cols - 3))
    sizes = [2, 2, 4, 4]
    chunks = []
    for size in sizes:
        if len(inner) > size:
            chunks.append(inner[:size])
            inner = inner[size:]
    if inner:
        chunks.append(inner)
    chunks.append([0, 1, 2, cols - 3, cols - 2, cols - 1])
    return chunks


def remote(src, dst, s, r, target):
    copy = pltpu.make_async_remote_copy(
        src_ref=src, dst_ref=dst, send_sem=s, recv_sem=r, device_id=target, device_id_type=MESH
    )
    copy.start()
    return copy


def main_kernel(n_lon, n_ens, cin, hid, chunks, *refs):
    (part_ref, obs_ref, prec_ref, stat_ref, anc_ref, temp_ref, win_ref, wmid_ref, wout_ref,
     out_ref, spare_ref, info_ref, wts_ref,
     raw, raw_obs, ext, obs_cm, a1, a2, w1, w2, w3, gain, misfit, anc_all, k_own, k_all,
     lon_sum, lon_parts, dom_parts, *rest) = refs
    n = len(chunks)
    mine, gathered, arrived = rest[:n], rest[n : 2 * n], rest[2 * n : 3 * n]
    (load_sem, anc_s, anc_r, halo_s, halo_r, sib_s, sib_r, x_s, x_r, fwd_s, fwd_r,
     lon_s, lon_r, dom_s, dom_r, ens_s, ens_r) = rest[3 * n :]
    slots, nvars, cols, lat = part_ref.shape
    rows = spare_ref.shape[2]
    f32, bf16 = jnp.float32, jnp.bfloat16

    dom, lon, ens = lax.axis_index("dom"), lax.axis_index("lon"), lax.axis_index("ens")
    core, chip = lax.rem(dom, 2), lax.div(dom, 2)
    sibling, partner = {"dom": dom + 1 - 2 * core}, {"dom": lax.rem(dom + 2, 4)}

    def lon_at(k):
        return {"lon": lax.rem(lon + k, n_lon)}

    def dom_at(k):
        return {"dom": lax.rem(dom + k, 4)}

    def ens_at(k):
        return {"ens": lax.rem(ens + k, n_ens)}

    peers = [dom_at(k) for k in range(1, 4)] + [lon_at(k) for k in range(1, n_lon)]
    peers += [ens_at(k) for k in range(1, n_ens)]
    barrier = pltpu.get_barrier_semaphore()
    for peer in peers:
        pl.semaphore_signal(barrier, inc=1, device_id=peer, device_id_type=MESH)

    loads = [pltpu.make_async_copy(part_ref.at[p], raw.at[p], load_sem.at[p]) for p in range(slots)]
    loads.append(pltpu.make_async_copy(obs_ref, raw_obs, load_sem.at[slots]))
    for load in loads:
        load.start()

    w1[...] = jnp.zeros_like(w1)
    w3[...] = jnp.zeros_like(w3)
    for j in range(3):
        for i in range(3):
            w1[j * hid : (j + 1) * hid, i * cin : i * cin + nvars] = win_ref[i, j]
            w2[j * hid : (j + 1) * hid, i * hid : (i + 1) * hid] = wmid_ref[i, j]
            turned = wout_ref[i, j].astype(f32).T
            w3[j * cin : j * cin + nvars, i * hid : (i + 1) * hid] = turned.astype(bf16)
    gain[...] = 0.25 * (stat_ref[...].astype(f32) * prec_ref[...])
    misfit[...] = jnp.zeros_like(misfit)

    pl.semaphore_wait(barrier, len(peers))
    for s in range(slots):
        anc_all[dom, s] = anc_ref[s]
    sent_anc = [
        remote(anc_ref, anc_all.at[dom], anc_s.at[k - 1], anc_r.at[k - 1], dom_at(k))
        for k in range(1, 4)
    ]

    def turn(src, dst, at, x0):
        width = 8
        for q in range(0, cin, 16):
            count = min(16, nvars - q)
            v = src[q : q + count, x0 : x0 + width, :].astype(f32)
            if count < 16:
                v = jnp.concatenate([v, jnp.zeros((16 - count, width, lat), f32)], axis=0)
            dst[at + x0 : at + x0 + width, q : q + 16, :] = jnp.swapaxes(v, 0, 1).astype(bf16)

    for p in range(slots):
        loads[p].wait()
        turn(raw.at[p], ext.at[p], 3, 0)
        turn(raw.at[p], ext.at[p], 3, cols - 8)
    halos = [
        remote(ext.at[:, cols : cols + 3], ext.at[:, 0:3], halo_s.at[0], halo_r.at[0], lon_at(1)),
        remote(ext.at[:, 3:6], ext.at[:, cols + 3 : cols + 6], halo_s.at[1], halo_r.at[1], lon_at(n_lon - 1)),
    ]
    for p in range(slots):
        for x0 in range(8, cols - 8, 8):
            turn(raw.at[p], ext.at[p], 3, x0)
    loads[slots].wait()
    for x0 in range(0, cols, 8):
        turn(raw_obs, obs_cm, 0, x0)

    lane_h = lax.broadcasted_iota(jnp.int32, (hid, lat), 1)
    lane_o = lax.broadcasted_iota(jnp.int32, (cin, lat), 1)
    edges_h = (lane_h == 0, lane_h == lat - 1)
    edges_o = (lane_o == 0, lane_o == lat - 1)

    def conv(src, w, x, out_rows, edges):
        window = src[x : x + 3]
        window = window.reshape(window.shape[0] * window.shape[1], lat)
        v = jnp.dot(w[...], window, preferred_element_type=f32)
        below = pltpu.roll(v[:out_rows], 1, 1)
        above = pltpu.roll(v[2 * out_rows :], lat - 1, 1)
        return (
            v[out_rows : 2 * out_rows]
            + jnp.where(edges[0], 0.0, below)
            + jnp.where(edges[1], 0.0, above)
        )

    def first(p, x):
        a1[p, x + 2] = silu(conv(ext.at[p], w1, x + 2, hid, edges_h)).astype(bf16)

    def second(p, x):
        a2[p, x + 1] = silu(conv(a1.at[p], w2, x + 1, hid, edges_h)).astype(bf16)

    def third(p, x, dst, at):
        noise = conv(a2.at[p], w3, x, cin, edges_o)
        current = ext[p, x + 3].astype(f32)
        diff = obs_cm[x].astype(f32) - current
        pull = gain[x : x + 1, :] * diff
        new = current - 0.5 * noise + pull
        dst[p, at] = new[:rows].astype(bf16)
        square = pull * diff
        total = square[0:8]
        for r in range(8, cin, 8):
            total = total + square[r : r + 8]
        misfit[p] += total

    def share(c):
        return remote(mine[c].at[0:slots], mine[c].at[slots : 2 * slots], sib_s.at[c], sib_r.at[c], sibling)

    def choose():
        theirs = [anc_all[2 * (1 - chip) + i, s] for i in range(2) for s in range(slots)]
        ours = [anc_all[2 * chip + i, s] for i in range(2) for s in range(slots)]
        group = 2 * slots
        one, zero = jnp.int32(1), jnp.int32(0)

        def wanted(ids, base):
            flags = []
            for r in range(group):
                flag = zero
                for g in ids:
                    flag = jnp.where(g == base + r, one, flag)
                flags.append(flag)
            return flags

        give = wanted(theirs, group * chip)
        take = wanted(ours, group * (1 - chip))
        order, count = [zero] * group, zero
        for r in range(group):
            for j in range(r + 1):
                order[j] = jnp.where((count == j) & (give[r] == 1), jnp.int32(r), order[j])
            count = count + give[r]
        near = [jnp.where(lax.div(r, slots) == core, zero, jnp.int32(slots)) + lax.rem(r, slots) for r in order]
        ranks, got = [], zero
        for r in range(group):
            ranks.append(got)
            got = got + take[r]
        sources = []
        for s in range(slots):
            g = anc_ref[s]
            r = g - group * lax.div(g, group)
            rank = zero
            for m in range(group):
                rank = jnp.where(r == m, ranks[m], rank)
            local = jnp.where(lax.div(r, slots) == core, zero, jnp.int32(slots)) + lax.rem(r, slots)
            sources.append(jnp.where(lax.div(g, group) == chip, local, group + rank))
        return near, sources, jnp.maximum(count, got)

    state = {}

    def pass_on(c, shared):
        if not state:
            for copy in sent_anc:
                copy.wait()
            near, sources, most = choose()
            k_own[0] = most
            state["near"], state["sources"] = near, sources
            state["ens"] = [
                remote(k_own, k_all.at[k - 1], ens_s.at[k - 1], ens_r.at[k - 1], ens_at(k))
                for k in range(1, n_ens)
            ]
        shared.wait()
        half = len(chunks[c]) // 2
        start = core * half
        for j in range(FIXED):
            for t in range(half):
                gathered[c][j, t] = mine[c][state["near"][j], start + t]
        base = sum(len(chunk) for chunk in chunks[:c]) // 2
        for j in range(FIXED, 2 * slots):
            for t in range(half):
                spare_ref[j - FIXED, base + t] = mine[c][state["near"][j], start + t]
        return remote(gathered[c], arrived[c].at[core], x_s.at[c], x_r.at[c], partner)

    done = {"first": None, "second": None}
    crossings, waiting = [], None
    for c, chunk in enumerate(chunks):
        if c == n - 1:
            for halo in halos:
                halo.wait()
            one = list(range(-2, 1)) + list(range(cols - 1, cols + 2))
            two = list(range(-1, 2)) + list(range(cols - 2, cols + 1))
        else:
            lo, hi = chunk[0], chunk[-1]
            one = [x for x in range(lo - 2, hi + 3) if c == 0 or x > chunks[c - 1][-1] + 2]
            two = [x for x in range(lo - 1, hi + 2) if c == 0 or x > chunks[c - 1][-1] + 1]
        for x in one:
            for p in range(slots):
                first(p, x)
        for x in two:
            for p in range(slots):
                second(p, x)
        for at, x in enumerate(chunk):
            for p in range(slots):
                third(p, x, mine[c], at)
        shared = share(c)
        if waiting is not None:
            crossings.append(pass_on(c - 1, waiting))
        waiting = shared
    crossings.append(pass_on(n - 1, waiting))

    sums = [jnp.sum(misfit[p], axis=0, keepdims=True) for p in range(slots)]
    sums = [s[:, :128] + s[:, 128:] for s in sums]
    row = lax.broadcasted_iota(jnp.int32, (8, 128), 0)
    local = jnp.zeros((8, 128), f32)
    for p in range(slots):
        local = jnp.where(row == p, sums[p], local)
    lon_sum[...] = 4.0 * local
    sent = [
        remote(lon_sum, lon_parts.at[k - 1], lon_s.at[k - 1], lon_r.at[k - 1], lon_at(k))
        for k in range(1, n_lon)
    ]
    for copy in sent:
        copy.wait()
    band = lon_sum[...]
    for k in range(1, n_lon):
        band = band + lon_parts[k - 1]
    dom_parts[0] = band
    sent = [
        remote(dom_parts.at[0], dom_parts.at[k], dom_s.at[k - 1], dom_r.at[k - 1], dom_at(k))
        for k in range(1, 4)
    ]

    forwards = []

    def finish(c):
        forwards[c].wait()
        half = len(chunks[c]) // 2
        for s in range(slots):
            src = state["sources"][s]
            near = jnp.minimum(src, 2 * slots - 1)
            far = jnp.clip(src - 2 * slots, 0, FIXED - 1)
            for at, x in enumerate(chunks[c]):
                out_ref[s, x] = jnp.where(
                    src < 2 * slots, mine[c][near, at], arrived[c][at // half, far, at % half]
                )[:nvars]

    for c in range(n):
        crossings[c].wait()
        forwards.append(
            remote(arrived[c].at[core], arrived[c].at[core], fwd_s.at[c], fwd_r.at[c], sibling)
        )
        if c == 0:
            for copy in sent:
                copy.wait()
            misfits = [jnp.broadcast_to(jnp.sum(dom_parts[k], axis=1, keepdims=True), (8, 128)) for k in range(4)]
            real = row < slots

            def over(values):
                total = values[0]
                for value in values[1:]:
                    total = total + value
                return jnp.sum(jnp.where(real, total, 0.0), axis=0, keepdims=True)

            center = over(misfits) / (4 * slots)
            off = [m - center for m in misfits]
            spread = jnp.sqrt(over([d * d for d in off]) / (4 * slots) + 1.0)
            expos = [jnp.exp(-0.5 * temp_ref[0] * d / spread) for d in off]
            wts_ref[...] = expos[0] / over(expos)
        if c > 0:
            finish(c - 1)
    finish(n - 1)

    most = k_own[0]
    for copy in state["ens"]:
        copy.wait()
    for k in range(1, n_ens):
        most = jnp.maximum(most, k_all[k - 1, 0])
    info_ref[0] = jnp.maximum(most - FIXED, 0)
    for s in range(slots):
        info_ref[1 + s] = state["sources"][s]


def main_call(particles, observed, precision, stations, ancestors, tempering, w_in, w_mid, w_out):
    slots, nvars, cols, lat = particles.shape
    hid = w_mid.shape[2]
    cin, rows = pad_to(nvars, 16), pad_to(nvars, 8)
    n_lon, n_ens = lax.axis_size("lon"), lax.axis_size("ens")
    chunks = column_chunks(cols)
    n = len(chunks)
    bf16, f32 = jnp.bfloat16, jnp.float32
    vmem = pl.BlockSpec(memory_space=pltpu.VMEM)
    smem = pl.BlockSpec(memory_space=pltpu.SMEM)
    hbm = pl.BlockSpec(memory_space=pltpu.HBM)
    dma = pltpu.SemaphoreType.DMA
    scratch = [
        pltpu.VMEM((slots, nvars, cols, lat), bf16),
        pltpu.VMEM((nvars, cols, lat), bf16),
        pltpu.VMEM((slots, cols + 6, cin, lat), bf16),
        pltpu.VMEM((cols, cin, lat), bf16),
        pltpu.VMEM((slots, cols + 4, hid, lat), bf16),
        pltpu.VMEM((slots, cols + 2, hid, lat), bf16),
        pltpu.VMEM((3 * hid, 3 * cin), bf16),
        pltpu.VMEM((3 * hid, 3 * hid), bf16),
        pltpu.VMEM((3 * cin, 3 * hid), bf16),
        pltpu.VMEM((cols, lat), f32),
        pltpu.VMEM((slots, 8, lat), f32),
        pltpu.SMEM((4, slots), jnp.int32),
        pltpu.SMEM((1,), jnp.int32),
        pltpu.SMEM((max(n_ens - 1, 1), 1), jnp.int32),
        pltpu.VMEM((8, 128), f32),
        pltpu.VMEM((max(n_lon - 1, 1), 8, 128), f32),
        pltpu.VMEM((4, 8, 128), f32),
    ]
    scratch += [pltpu.VMEM((2 * slots, len(c), rows, lat), bf16) for c in chunks]
    scratch += [pltpu.VMEM((FIXED, len(c) // 2, rows, lat), bf16) for c in chunks]
    scratch += [pltpu.VMEM((2, FIXED, len(c) // 2, rows, lat), bf16) for c in chunks]
    scratch += [dma((slots + 1,))] + [dma((3,))] * 2 + [dma((2,))] * 2 + [dma((n,))] * 6
    scratch += [dma((max(n_lon - 1, 1),))] * 2 + [dma((3,))] * 2 + [dma((max(n_ens - 1, 1),))] * 2
    return pl.pallas_call(
        functools.partial(main_kernel, n_lon, n_ens, cin, hid, chunks),
        out_shape=(
            jax.ShapeDtypeStruct((slots, cols, nvars, lat), bf16),
            jax.ShapeDtypeStruct((2 * slots - FIXED, cols // 2, rows, lat), bf16),
            jax.ShapeDtypeStruct((1 + slots,), jnp.int32),
            jax.ShapeDtypeStruct((8, 128), f32),
        ),
        in_specs=[hbm, hbm, vmem, vmem, smem, smem, vmem, vmem, vmem],
        out_specs=(vmem, vmem, smem, vmem),
        scratch_shapes=scratch,
        compiler_params=pltpu.CompilerParams(
            collective_id=0, has_side_effects=True, vmem_limit_bytes=48 << 20
        ),
        name="step",
    )(particles, observed, precision, stations, ancestors, tempering, w_in, w_mid, w_out.transpose(0, 1, 3, 2))


def more_kernel(extra, chunks, info_ref, out_in, spare_ref, out_ref, arrived, x_s, x_r, fwd_s, fwd_r):
    slots = out_in.shape[0]
    nvars = out_in.shape[2]
    dom = lax.axis_index("dom")
    core = lax.rem(dom, 2)
    sibling, partner = {"dom": dom + 1 - 2 * core}, {"dom": lax.rem(dom + 2, 4)}
    barrier = pltpu.get_barrier_semaphore()
    for peer in (sibling, partner):
        pl.semaphore_signal(barrier, inc=1, device_id=peer, device_id_type=MESH)
    pl.semaphore_wait(barrier, 2)
    spans, at = [], 0
    for chunk in chunks:
        spans.append((at, len(chunk) // 2))
        at += len(chunk) // 2
    crossings = []
    for j in range(extra):
        for c, (lo, size) in enumerate(spans):
            i = j * len(spans) + c
            crossings.append(remote(
                spare_ref.at[j, pl.ds(lo, size)], arrived.at[core, j, pl.ds(lo, size)],
                x_s.at[i], x_r.at[i], partner,
            ))
    forwards = []
    for j in range(extra):
        for c, (lo, size) in enumerate(spans):
            i = j * len(spans) + c
            crossings[i].wait()
            piece = arrived.at[core, j, pl.ds(lo, size)]
            forwards.append(remote(piece, piece, fwd_s.at[i], fwd_r.at[i], sibling))
    for copy in forwards:
        copy.wait()
    for s in range(slots):
        src = info_ref[1 + s]
        far = jnp.clip(src - (2 * slots + FIXED), 0, extra - 1)
        for chunk, (lo, size) in zip(chunks, spans):
            for at, x in enumerate(chunk):
                out_ref[s, x] = jnp.where(
                    src < 2 * slots + FIXED, out_in[s, x], arrived[at // size, far, lo + at % size][:nvars]
                )


def more_call(extra, info, out, spare):
    slots, cols, nvars, lat = out.shape
    chunks = column_chunks(cols)
    vmem = pl.BlockSpec(memory_space=pltpu.VMEM)
    dma = pltpu.SemaphoreType.DMA
    return pl.pallas_call(
        functools.partial(more_kernel, extra, chunks),
        out_shape=jax.ShapeDtypeStruct(out.shape, out.dtype),
        in_specs=[pl.BlockSpec(memory_space=pltpu.SMEM), vmem, vmem],
        out_specs=vmem,
        scratch_shapes=[pltpu.VMEM((2, extra) + spare.shape[1:], out.dtype)] + [dma((extra * len(chunks),))] * 4,
        compiler_params=pltpu.CompilerParams(
            collective_id=extra, has_side_effects=True, vmem_limit_bytes=24 << 20
        ),
        name="more",
    )(info, out, spare)


def two_chips(*args):
    out, spare, info, weights = main_call(*args)
    slots = out.shape[0]
    branches = [lambda info, out, spare: out]
    for extra in range(1, 2 * slots - FIXED + 1):
        branches.append(functools.partial(more_call, extra))
    out = lax.switch(info[0], branches, info, out, spare)
    return (out.transpose(0, 2, 1, 3), weights[:slots, 0])


def on_device(*args):
    if lax.axis_size("dom") == 4 and args[0].shape[2] >= 16:
        return two_chips(*args)
    return many_chips(*args)


def solution(mesh):
    return jax.shard_map(
        on_device,
        mesh=mesh,
        in_specs=(
            P(("ens", "dom"), None, "lon", None),
            P("ens", "lon", None),
            P(("ens", "lon"), None),
            P(("ens", "lon"), None),
            P(("ens", "dom")),
            P("ens"),
            P(),
            P(),
            P(),
        ),
        out_specs=(P(("ens", "dom"), None, "lon", None), P(("ens", "dom"))),
        check_vma=False,
    )
```

```python
import functools

import jax
import jax.numpy as jnp
from jax import lax
from jax.experimental import pallas as pl
from jax.experimental.pallas import tpu as pltpu
from jax.sharding import PartitionSpec as P


def pad_to(count, step):
    return -(-count // step) * step


def stacked_taps(weight, out_rows, in_rows):
    _, _, outs, ins = weight.shape
    w = jnp.pad(weight, ((0, 0), (0, 0), (0, out_rows - outs), (0, in_rows - ins)))
    return w.transpose(1, 2, 0, 3).reshape(3 * out_rows, 3 * in_rows)


def conv_column(src_ref, w, x, in_rows, out_rows, first, last):
    window = src_ref[x * in_rows : (x + 3) * in_rows, :]
    p = jnp.dot(w, window, preferred_element_type=jnp.float32)
    lat = p.shape[1]
    below = pltpu.roll(p[:out_rows], 1, 1)
    above = pltpu.roll(p[2 * out_rows :], lat - 1, 1)
    return (
        p[out_rows : 2 * out_rows]
        + jnp.where(first, 0.0, below)
        + jnp.where(last, 0.0, above)
    )


def silu(v):
    half = 0.5 * v
    return half + half * jnp.tanh(half)


def step_kernel(spans, cin, hid, edges, *refs):
    if edges:
        low_ref, high_ref, *refs = refs
    mid_ref, obs_ref, ow_ref, w1_ref, w2_ref, w3_ref, out_ref, ext, a1, a2 = refs
    cols, nvars, lat = mid_ref.shape[1:]
    lane_h = lax.broadcasted_iota(jnp.int32, (hid, lat), 1)
    lane_o = lax.broadcasted_iota(jnp.int32, (cin, lat), 1)
    first_h, last_h = lane_h == 0, lane_h == lat - 1
    first_o, last_o = lane_o == 0, lane_o == lat - 1

    @pl.when(pl.program_id(0) == 0)
    def _():
        ext[...] = jnp.zeros_like(ext)

    at = 0
    for s, (lo, hi) in enumerate(spans):
        for k, x in enumerate(range(lo - 3, hi + 3)):
            if x < 0:
                column = low_ref[0, x + 3]
            elif x >= cols:
                column = high_ref[0, x - cols]
            else:
                column = mid_ref[0, x]
            ext[s, k * cin : k * cin + nvars, :] = column
        for x in range(hi - lo + 4):
            v = conv_column(ext.at[s], w1_ref[...], x, cin, hid, first_h, last_h)
            a1[s, x * hid : (x + 1) * hid, :] = silu(v).astype(jnp.bfloat16)
        for x in range(hi - lo + 2):
            v = conv_column(a1.at[s], w2_ref[...], x, hid, hid, first_h, last_h)
            a2[s, x * hid : (x + 1) * hid, :] = silu(v).astype(jnp.bfloat16)
        for x in range(hi - lo):
            noise = conv_column(a2.at[s], w3_ref[...], x, hid, cin, first_o, last_o)[:nvars]
            current = ext[s, (x + 3) * cin : (x + 4) * cin, :].astype(jnp.float32)[:nvars]
            seen = obs_ref[lo + x].astype(jnp.float32)
            gain = 0.25 * ow_ref[lo + x]
            new = current - 0.5 * noise + gain * (seen - current)
            out_ref[0, at] = new.astype(jnp.bfloat16)
            at += 1


def update_chunk(spans, edges, mid, observed, obs_weight, w1, w2, w3, cin, hid):
    slots, _, nvars, lat = mid.shape
    step = sum(hi - lo for lo, hi in spans)
    widest = max(hi - lo for lo, hi in spans)
    whole = lambda a: pl.BlockSpec(a.shape, lambda p: (0,) * a.ndim)
    own = lambda a: pl.BlockSpec((1,) + a.shape[1:], lambda p: (p, 0, 0, 0))
    return pl.pallas_call(
        functools.partial(step_kernel, spans, cin, hid, bool(edges)),
        out_shape=jax.ShapeDtypeStruct((slots, step, nvars, lat), jnp.bfloat16),
        grid=(slots,),
        in_specs=[own(a) for a in (*edges, mid)]
        + [whole(a) for a in (observed, obs_weight, w1, w2, w3)],
        out_specs=pl.BlockSpec((1, step, nvars, lat), lambda p: (p, 0, 0, 0)),
        scratch_shapes=[
            pltpu.VMEM((len(spans), (widest + 6) * cin, lat), jnp.bfloat16),
            pltpu.VMEM((len(spans), (widest + 4) * hid, lat), jnp.bfloat16),
            pltpu.VMEM((len(spans), (widest + 2) * hid, lat), jnp.bfloat16),
        ],
        compiler_params=pltpu.CompilerParams(vmem_limit_bytes=56 << 20),
        cost_estimate=pl.CostEstimate(flops=0, bytes_accessed=1024, transcendentals=0),
        name="update_chunk",
    )(*edges, mid, observed, obs_weight, w1, w2, w3)


def exchange_kernel(n_lon, mid_ref, sums_ref, low_ref, high_ref, total_ref, parts, edge_send, edge_recv, lon_send, lon_recv):
    lon = lax.axis_index("lon")
    cols = mid_ref.shape[1]

    def lon_at(k):
        return {"lon": lax.rem(lon + k, n_lon)}

    barrier = pltpu.get_barrier_semaphore()
    for k in range(1, n_lon):
        pl.semaphore_signal(barrier, inc=1, device_id=lon_at(k), device_id_type=pl.DeviceIdType.MESH)
    pl.semaphore_wait(barrier, n_lon - 1)

    def send(src, dst, s, r, target):
        copy = pltpu.make_async_remote_copy(
            src_ref=src, dst_ref=dst, send_sem=s, recv_sem=r,
            device_id=target, device_id_type=pl.DeviceIdType.MESH,
        )
        copy.start()
        return copy

    edges = [
        send(mid_ref.at[:, cols - 3 : cols], low_ref, edge_send.at[0], edge_recv.at[0], lon_at(1)),
        send(mid_ref.at[:, 0:3], high_ref, edge_send.at[1], edge_recv.at[1], lon_at(n_lon - 1)),
    ]
    parts[lon] = sums_ref[...]
    over_lon = [
        send(sums_ref, parts.at[lon], lon_send.at[k - 1], lon_recv.at[k - 1], lon_at(k))
        for k in range(1, n_lon)
    ]
    for copy in over_lon:
        copy.wait()
    band_sum = parts[0]
    for k in range(1, n_lon):
        band_sum = band_sum + parts[k]
    total_ref[...] = band_sum
    for copy in edges:
        copy.wait()


def exchange(mid, sums, n_lon):
    slots, _, nvars, lat = mid.shape
    edge = jax.ShapeDtypeStruct((slots, 3, nvars, lat), mid.dtype)
    vmem = pl.BlockSpec(memory_space=pltpu.VMEM)
    return pl.pallas_call(
        functools.partial(exchange_kernel, n_lon),
        out_shape=(edge, edge, jax.ShapeDtypeStruct(sums.shape, jnp.float32)),
        in_specs=[pl.BlockSpec(memory_space=pl.ANY), vmem],
        out_specs=(vmem, vmem, vmem),
        scratch_shapes=[
            pltpu.VMEM((n_lon,) + sums.shape, jnp.float32),
            pltpu.SemaphoreType.DMA((2,)),
            pltpu.SemaphoreType.DMA((2,)),
            pltpu.SemaphoreType.DMA((n_lon - 1,)),
            pltpu.SemaphoreType.DMA((n_lon - 1,)),
        ],
        compiler_params=pltpu.CompilerParams(collective_id=0, has_side_effects=True),
        cost_estimate=pl.CostEstimate(flops=0, bytes_accessed=1024, transcendentals=0),
        name="exchange",
    )(mid, sums)


def across(u):
    n = lax.axis_size("dom")
    return [u] + [
        lax.ppermute(u, "dom", [(d, (d + 2 * k) % n) for d in range(n)]) for k in range(1, n // 2)
    ]


def pick_kernel(slots, base, codes_ref, *refs):
    *pieces, out_ref = refs
    if base == 0:
        received_ref, *pieces = pieces
    for s in range(slots):
        for m in range(len(pieces) * slots):
            wanted = codes_ref[base + s] == m
            if base == 0:
                wanted = wanted & (codes_ref[2 * slots + s] == 1)

            @pl.when(wanted)
            def _():
                out_ref[s] = pieces[m // slots][m % slots]

        if base == 0:

            @pl.when(codes_ref[2 * slots + s] == 0)
            def _():
                out_ref[s] = received_ref[s]


def pick(codes, base, arrays):
    u = arrays[0]
    slots = u.shape[0]
    vmem = pl.BlockSpec(memory_space=pltpu.VMEM)
    return pl.pallas_call(
        functools.partial(pick_kernel, slots, base),
        out_shape=jax.ShapeDtypeStruct(u.shape, u.dtype),
        in_specs=[pl.BlockSpec(memory_space=pltpu.SMEM)] + [vmem] * len(arrays),
        out_specs=vmem,
        compiler_params=pltpu.CompilerParams(vmem_limit_bytes=24 << 20),
        cost_estimate=pl.CostEstimate(flops=0, bytes_accessed=1024, transcendentals=0),
        name="pick",
    )(codes, *arrays)


def weight_kernel(slots, t_ref, *refs):
    *part_refs, out_ref = refs
    shape = out_ref.shape
    real = lax.broadcasted_iota(jnp.int32, shape, 0) < slots
    count = len(part_refs) * slots

    def over_particles(rows):
        total = rows[0]
        for row in rows[1:]:
            total = total + row
        return jnp.sum(total, axis=0, keepdims=True)

    misfits = [jnp.broadcast_to(jnp.sum(r[...], axis=1, keepdims=True), shape) for r in part_refs]
    center = over_particles([jnp.where(real, m, 0.0) for m in misfits]) / count
    deviations = [jnp.where(real, m - center, 0.0) for m in misfits]
    spread = jnp.sqrt(over_particles([d * d for d in deviations]) / count + 1.0)
    expos = [jnp.where(real, jnp.exp(-0.5 * t_ref[0] * d / spread), 0.0) for d in deviations]
    out_ref[...] = expos[0] / over_particles(expos)


def own_weights_of(parts, tempering, slots):
    vmem = pl.BlockSpec(memory_space=pltpu.VMEM)
    out = pl.pallas_call(
        functools.partial(weight_kernel, slots),
        out_shape=jax.ShapeDtypeStruct(parts[0].shape, jnp.float32),
        in_specs=[pl.BlockSpec(memory_space=pltpu.SMEM)] + [vmem] * len(parts),
        out_specs=vmem,
        name="own_weights",
    )(tempering, *parts)
    return out[:slots, 0]


def many_chips(particles, observed, precision, stations, ancestors, tempering, w_in, w_mid, w_out):
    slots, nvars, cols, lat = particles.shape
    hid = w_mid.shape[2]
    cin = pad_to(nvars, 16)
    n_dom, n_lon = lax.axis_size("dom"), lax.axis_size("lon")
    me = lax.axis_index("dom")
    mid = particles.transpose(0, 2, 1, 3)
    sibling_anc = lax.ppermute(ancestors, "dom", [(d, d ^ 1) for d in range(n_dom)])

    obs_weight = stations.astype(jnp.float32) * precision
    wanted = jnp.concatenate([ancestors, sibling_anc])
    owner = lax.div(wanted, slots)
    chips = n_dom // 2
    steps = lax.rem(lax.shift_right_logical(me, 1) - lax.div(owner, 2) + chips, chips)
    candidate = steps * slots + lax.rem(wanted, slots)
    here = lax.rem(owner, 2) == (me & 1)

    obs_columns = observed.transpose(1, 0, 2)
    ow_columns = obs_weight[:, None, :]
    w1 = stacked_taps(w_in, hid, cin)
    w2 = stacked_taps(w_mid, hid, hid)
    w3 = stacked_taps(w_out, cin, hid)

    update = lambda spans, edges: update_chunk(
        spans, edges, mid, obs_columns, ow_columns, w1, w2, w3, cin, hid
    )
    u = update([(3, cols - 3)], [])
    groups = [across(u)]

    late_weight, _ = lax.optimization_barrier((obs_weight, u))
    misfit_cell = particles.astype(jnp.float32) - observed.astype(jnp.float32)[None]
    local_sums = jnp.sum(late_weight[None, None] * misfit_cell * misfit_cell, axis=(1, 2))
    sums = jnp.sum(local_sums.reshape(slots, lat // 128, 128), axis=1)
    sums = jnp.pad(sums, ((0, pad_to(slots, 8) - slots), (0, 0)))
    low, high, band_sums = exchange(mid, sums, n_lon)
    groups.append(across(update([(0, 3), (cols - 3, cols)], [low, high])))

    parts = [band_sums] + [
        lax.ppermute(band_sums, "dom", [(d, (d + k) % n_dom) for d in range(n_dom)])
        for k in range(1, n_dom)
    ]
    own_weights = own_weights_of(parts, tempering, slots)

    codes = jnp.concatenate([candidate, here[:slots].astype(jnp.int32)])
    groups = lax.optimization_barrier(groups)
    results = []
    for pieces in groups:
        sent = pick(codes, slots, pieces)
        received = lax.ppermute(sent, "dom", [(d, d ^ 1) for d in range(n_dom)])
        results.append(pick(codes, 0, [received, *pieces]))
    inner, sides = results
    new_columns = jnp.concatenate([sides[:, :3], inner, sides[:, 3:]], axis=1)
    return (new_columns.transpose(0, 2, 1, 3), own_weights)


MESH = pl.DeviceIdType.MESH
FIXED = 2


def column_chunks(cols):
    middle = cols // 2
    chunks = [[middle - 1, middle]]
    above, below = list(range(middle + 1, cols - 3)), list(range(3, middle - 1))
    for side, take in ((above, lambda v, k: v[:k]), (below, lambda v, k: v[-k:])):
        left = side
        while left:
            size = 4 if len(left) >= 6 or len(left) == 4 else min(len(left), 6)
            part = take(left, size)
            chunks.append(part)
            left = [x for x in left if x not in part]
    chunks.append([0, 1, 2, cols - 3, cols - 2, cols - 1])
    return chunks


def remote(src, dst, s, r, target):
    copy = pltpu.make_async_remote_copy(
        src_ref=src, dst_ref=dst, send_sem=s, recv_sem=r, device_id=target, device_id_type=MESH
    )
    copy.start()
    return copy


def main_kernel(n_lon, n_ens, cin, hid, chunks, *refs):
    (part_hbm, obs_hbm, prec_hbm, stat_hbm, anc_hbm, temp_hbm, win_hbm, wmid_hbm, wout_hbm,
     out_ref, spare_ref, info_ref, wts_ref,
     raw, raw_obs, prec_ref, stat_ref, anc_ref, temp_ref, win_ref, wmid_ref, wout_ref, ext, obs_cm, a1, a2, w1, w2, w3, gain, misfit, anc_own, anc_all, k_own, k_all,
     lon_sum, lon_parts, dom_parts, *rest) = refs
    n = len(chunks)
    mine, gathered, arrived = rest[:n], rest[n : 2 * n], rest[2 * n : 3 * n]
    (load_sem, anc_s, anc_r, halo_s, halo_r, sib_s, sib_r, x_s, x_r, fwd_s, fwd_r,
     lon_s, lon_r, dom_s, dom_r, ens_s, ens_r, from_low, from_high) = rest[3 * n :]
    slots, nvars, cols, lat = part_hbm.shape
    rows = spare_ref.shape[2]
    f32, bf16 = jnp.float32, jnp.bfloat16

    dom, lon, ens = lax.axis_index("dom"), lax.axis_index("lon"), lax.axis_index("ens")
    core, chip = lax.rem(dom, 2), lax.div(dom, 2)
    sibling, partner = {"dom": dom + 1 - 2 * core}, {"dom": lax.rem(dom + 2, 4)}

    def lon_at(k):
        return {"lon": lax.rem(lon + k, n_lon)}

    def dom_at(k):
        return {"dom": lax.rem(dom + k, 4)}

    def ens_at(k):
        return {"ens": lax.rem(ens + k, n_ens)}

    peers = [dom_at(k) for k in range(1, 4)] + [ens_at(k) for k in range(1, n_ens)]
    barrier = pltpu.get_barrier_semaphore()
    for peer in peers:
        pl.semaphore_signal(barrier, inc=1, device_id=peer, device_id_type=MESH)

    @pl.when(lon < n_lon - 1)
    def _():
        pl.semaphore_signal(barrier, inc=1, device_id=lon_at(1), device_id_type=MESH)

    @pl.when(lon > 0)
    def _():
        pl.semaphore_signal(barrier, inc=1, device_id=lon_at(n_lon - 1), device_id_type=MESH)

    def load(src, dst, i):
        copy = pltpu.make_async_copy(src, dst, load_sem.at[i])
        copy.start()
        return copy

    names = [
        (anc_hbm, anc_ref), (win_hbm, win_ref), (wmid_hbm, wmid_ref), (wout_hbm, wout_ref),
        (prec_hbm, prec_ref), (stat_hbm, stat_ref), (temp_hbm, temp_ref),
    ]
    small = [load(src, dst, slots + 1 + i) for i, (src, dst) in enumerate(names)]
    states = [load(part_hbm.at[p], raw.at[p], p) for p in range(slots)]
    seen = load(obs_hbm, raw_obs, slots)

    w1[...] = jnp.zeros_like(w1)
    w3[...] = jnp.zeros_like(w3)
    misfit[...] = jnp.zeros_like(misfit)
    small[0].wait()
    for s in range(slots):
        anc_own[s] = anc_ref[s]
        anc_all[dom, s] = anc_ref[s]

    @pl.when((lon > 0) & (lon < n_lon - 1))
    def _():
        pl.semaphore_wait(barrier, len(peers) + 2)

    @pl.when((lon == 0) | (lon == n_lon - 1))
    def _():
        pl.semaphore_wait(barrier, len(peers) + 1)

    sent_anc = [
        remote(anc_own, anc_all.at[dom], anc_s.at[k - 1], anc_r.at[k - 1], dom_at(k))
        for k in range(1, 4)
    ]
    @pl.when(lon == 0)
    def _():
        pl.semaphore_signal(from_low, inc=1, device_id=lon_at(1), device_id_type=MESH)

    @pl.when(lon == n_lon - 1)
    def _():
        pl.semaphore_signal(from_high, inc=1, device_id=lon_at(n_lon - 1), device_id_type=MESH)

    def relay(r):
        @pl.when(lon == r)
        def _():
            pl.semaphore_wait(from_low, 1)
            if r < n_lon - 1:
                pl.semaphore_signal(from_low, inc=1, device_id=lon_at(1), device_id_type=MESH)

        @pl.when(lon == n_lon - 1 - r)
        def _():
            pl.semaphore_wait(from_high, 1)
            if r < n_lon - 1:
                pl.semaphore_signal(from_high, inc=1, device_id=lon_at(n_lon - 1), device_id_type=MESH)

    for copy in small[1:]:
        copy.wait()
    for j in range(3):
        for i in range(3):
            w1[j * hid : (j + 1) * hid, i * cin : i * cin + nvars] = win_ref[i, j]
            w2[j * hid : (j + 1) * hid, i * hid : (i + 1) * hid] = wmid_ref[i, j]
            turned = wout_ref[i, j].astype(f32).T
            w3[j * cin : j * cin + nvars, i * hid : (i + 1) * hid] = turned.astype(bf16)
    gain[...] = 0.25 * (stat_ref[...].astype(f32) * prec_ref[...])

    def turn(src, dst, at, x0):
        width = 8
        for q in range(0, cin, 16):
            count = min(16, nvars - q)
            v = src[q : q + count, x0 : x0 + width, :].astype(f32)
            if count < 16:
                v = jnp.concatenate([v, jnp.zeros((16 - count, width, lat), f32)], axis=0)
            dst[at + x0 : at + x0 + width, q : q + 16, :] = jnp.swapaxes(v, 0, 1).astype(bf16)

    middle = 8 * (cols // 16)
    outer = [x0 for x0 in range(0, cols, 8) if x0 != middle]
    for p in range(slots):
        states[p].wait()
        turn(raw.at[p], ext.at[p], 3, middle)
    seen.wait()
    turn(raw_obs, obs_cm, 0, middle)

    lane_h = lax.broadcasted_iota(jnp.int32, (hid, lat), 1)
    lane_o = lax.broadcasted_iota(jnp.int32, (cin, lat), 1)
    edges_h = (lane_h == 0, lane_h == lat - 1)
    edges_o = (lane_o == 0, lane_o == lat - 1)

    def conv(src, w, x, out_rows, edges):
        window = src[x : x + 3]
        window = window.reshape(window.shape[0] * window.shape[1], lat)
        v = jnp.dot(w[...], window, preferred_element_type=f32)
        below = pltpu.roll(v[:out_rows], 1, 1)
        above = pltpu.roll(v[2 * out_rows :], lat - 1, 1)
        return (
            v[out_rows : 2 * out_rows]
            + jnp.where(edges[0], 0.0, below)
            + jnp.where(edges[1], 0.0, above)
        )

    def first(p, x):
        a1[p, x + 2] = silu(conv(ext.at[p], w1, x + 2, hid, edges_h)).astype(bf16)

    def second(p, x):
        a2[p, x + 1] = silu(conv(a1.at[p], w2, x + 1, hid, edges_h)).astype(bf16)

    def third(p, x, dst, at):
        noise = conv(a2.at[p], w3, x, cin, edges_o)
        current = ext[p, x + 3].astype(f32)
        diff = obs_cm[x].astype(f32) - current
        pull = gain[x : x + 1, :] * diff
        new = current - 0.5 * noise + pull
        dst[p, at] = new[:rows].astype(bf16)
        square = pull * diff
        total = square[0:8]
        for r in range(8, cin, 8):
            total = total + square[r : r + 8]
        misfit[p] += total

    def share(c):
        return remote(mine[c].at[0:slots], mine[c].at[slots : 2 * slots], sib_s.at[c], sib_r.at[c], sibling)

    def choose():
        theirs = [anc_all[2 * (1 - chip) + i, s] for i in range(2) for s in range(slots)]
        ours = [anc_all[2 * chip + i, s] for i in range(2) for s in range(slots)]
        group = 2 * slots
        one, zero = jnp.int32(1), jnp.int32(0)

        def wanted(ids, base):
            flags = []
            for r in range(group):
                flag = zero
                for g in ids:
                    flag = jnp.where(g == base + r, one, flag)
                flags.append(flag)
            return flags

        give = wanted(theirs, group * chip)
        take = wanted(ours, group * (1 - chip))
        order, count = [zero] * group, zero
        for r in range(group):
            for j in range(r + 1):
                order[j] = jnp.where((count == j) & (give[r] == 1), jnp.int32(r), order[j])
            count = count + give[r]
        near = [jnp.where(lax.div(r, slots) == core, zero, jnp.int32(slots)) + lax.rem(r, slots) for r in order]
        ranks, got = [], zero
        for r in range(group):
            ranks.append(got)
            got = got + take[r]
        sources, remotes = [], []
        for s in range(slots):
            g = anc_ref[s]
            r = g - group * lax.div(g, group)
            rank = zero
            for m in range(group):
                rank = jnp.where(r == m, ranks[m], rank)
            local = jnp.where(lax.div(r, slots) == core, zero, jnp.int32(slots)) + lax.rem(r, slots)
            sources.append(jnp.where(lax.div(g, group) == chip, local, group + rank))
            remotes.append(r)
        return near, sources, remotes, jnp.maximum(count, got)

    state = {}

    def pass_on(c, shared):
        shared.wait()
        half = len(chunks[c]) // 2
        start = core * half
        for j in range(FIXED):
            for t in range(half):
                gathered[c][j, t] = mine[c][state["near"][j], start + t]
        base = sum(len(chunk) for chunk in chunks[1:c]) // 2
        for j in range(FIXED, 2 * slots):
            for t in range(half):
                spare_ref[j - FIXED, base + t] = mine[c][state["near"][j], start + t]
        return remote(gathered[c], arrived[c].at[core], x_s.at[c], x_r.at[c], partner)

    ready = [set(), set()]

    def compute(c):
        one = sorted({x + d for x in chunks[c] for d in range(-2, 3)} - ready[0])
        two = sorted({x + d for x in chunks[c] for d in range(-1, 2)} - ready[1])
        ready[0].update(one)
        ready[1].update(two)
        for x in one:
            for p in range(slots):
                first(p, x)
        for x in two:
            for p in range(slots):
                second(p, x)
        for at, x in enumerate(chunks[c]):
            for p in range(slots):
                third(p, x, mine[c], at)

    relay(1)
    compute(0)
    ends = pl.ds(core * slots, slots)
    crossings = [
        remote(mine[0].at[0:slots], arrived[0].at[ends], x_s.at[0], x_r.at[0], partner)
    ]

    for x0 in outer:
        for p in range(slots):
            turn(raw.at[p], ext.at[p], 3, x0)

    def edge(up, start):
        if up:
            src, dst, k, target = ext.at[:, cols : cols + 3], ext.at[:, 0:3], 0, lon_at(1)
        else:
            src, dst, k, target = ext.at[:, 3:6], ext.at[:, cols + 3 : cols + 6], 1, lon_at(n_lon - 1)
        copy = pltpu.make_async_remote_copy(
            src_ref=src, dst_ref=dst, send_sem=halo_s.at[k], recv_sem=halo_r.at[k],
            device_id=target, device_id_type=MESH,
        )
        if start:
            copy.start()
        return copy

    @pl.when(lon < n_lon - 1)
    def _():
        edge(True, True)

    @pl.when(lon > 0)
    def _():
        edge(False, True)

    shares = [share(0)]
    relay(2)
    for x0 in outer:
        turn(raw_obs, obs_cm, 0, x0)
    compute(1)
    shares.append(share(1))
    for r in range(3, n_lon):
        relay(r)

    @pl.when(lon == n_lon - 1)
    def _():
        edge(True, True)

    @pl.when(lon == 0)
    def _():
        edge(False, True)

    for copy in sent_anc:
        copy.wait()
    near, sources, remotes, most = choose()
    k_own[0] = most
    state["near"], state["sources"], state["remotes"] = near, sources, remotes
    state["ens"] = [
        remote(k_own, k_all.at[k - 1], ens_s.at[k - 1], ens_r.at[k - 1], ens_at(k))
        for k in range(1, n_ens)
    ]
    shares[0].wait()
    crossings.append(pass_on(1, shares[1]))
    compute(2)
    shares.append(share(2))
    crossings.append(pass_on(2, shares[2]))
    for c in range(3, n):
        if c == n - 1:
            edge(True, False).wait()
            edge(False, False).wait()
        compute(c)
        shares.append(share(c))
        if c > 3 and c < n - 1:
            crossings.append(pass_on(c - 1, shares[c - 1]))
        if c == n - 2:
            crossings.append(pass_on(c, shares[c]))
    crossings.append(pass_on(n - 1, shares[n - 1]))

    sums = [jnp.sum(misfit[p], axis=0, keepdims=True) for p in range(slots)]
    sums = [s[:, :128] + s[:, 128:] for s in sums]
    row = lax.broadcasted_iota(jnp.int32, (8, 128), 0)
    local = jnp.zeros((8, 128), f32)
    for p in range(slots):
        local = jnp.where(row == p, sums[p], local)
    lon_sum[...] = 4.0 * local
    sent = [
        remote(lon_sum, lon_parts.at[k - 1], lon_s.at[k - 1], lon_r.at[k - 1], lon_at(k))
        for k in range(1, n_lon)
    ]
    forwards = []

    def finish(c):
        forwards[c].wait()
        half = len(chunks[c]) // 2
        for s in range(slots):
            src = state["sources"][s]
            near = jnp.minimum(src, 2 * slots - 1)
            far = jnp.clip(src - 2 * slots, 0, FIXED - 1)
            for at, x in enumerate(chunks[c]):
                if c == 0:
                    far_away = arrived[c][state["remotes"][s], at]
                else:
                    far_away = arrived[c][at // half, far, at % half]
                out_ref[s, x] = jnp.where(src < 2 * slots, mine[c][near, at], far_away)[:nvars]

    for c in range(n):
        crossings[c].wait()
        piece = arrived[c].at[ends if c == 0 else core]
        forwards.append(remote(piece, piece, fwd_s.at[c], fwd_r.at[c], sibling))
        if c == n - 3:
            for copy in sent:
                copy.wait()
            band = lon_sum[...]
            for k in range(1, n_lon):
                band = band + lon_parts[k - 1]
            dom_parts[0] = band
            sent = [
                remote(dom_parts.at[0], dom_parts.at[k], dom_s.at[k - 1], dom_r.at[k - 1], dom_at(k))
                for k in range(1, 4)
            ]
        if c == n - 2:
            for copy in sent:
                copy.wait()
            misfits = [jnp.broadcast_to(jnp.sum(dom_parts[k], axis=1, keepdims=True), (8, 128)) for k in range(4)]
            real = row < slots

            def over(values):
                total = values[0]
                for value in values[1:]:
                    total = total + value
                return jnp.sum(jnp.where(real, total, 0.0), axis=0, keepdims=True)

            center = over(misfits) / (4 * slots)
            off = [m - center for m in misfits]
            spread = jnp.sqrt(over([d * d for d in off]) / (4 * slots) + 1.0)
            expos = [jnp.exp(-0.5 * temp_ref[0] * d / spread) for d in off]
            own = expos[0] / over(expos)
            lane = lax.broadcasted_iota(jnp.int32, (8, 128), 1)
            for s in range(slots):
                wts_ref[s] = jnp.sum(jnp.where((row == s) & (lane == 0), own, 0.0))
        if c > 0:
            finish(c - 1)
    finish(n - 1)

    most = k_own[0]
    for copy in state["ens"]:
        copy.wait()
    for k in range(1, n_ens):
        most = jnp.maximum(most, k_all[k - 1, 0])
    info_ref[0] = jnp.maximum(most - FIXED, 0)
    for s in range(slots):
        info_ref[1 + s] = state["sources"][s]


def main_call(particles, observed, precision, stations, ancestors, tempering, w_in, w_mid, w_out):
    slots, nvars, cols, lat = particles.shape
    hid = w_mid.shape[2]
    cin, rows = pad_to(nvars, 16), pad_to(nvars, 8)
    n_lon, n_ens = lax.axis_size("lon"), lax.axis_size("ens")
    chunks = column_chunks(cols)
    n = len(chunks)
    bf16, f32 = jnp.bfloat16, jnp.float32
    vmem = pl.BlockSpec(memory_space=pltpu.VMEM)
    smem = pl.BlockSpec(memory_space=pltpu.SMEM)
    hbm = pl.BlockSpec(memory_space=pltpu.HBM)
    dma = pltpu.SemaphoreType.DMA
    scratch = [
        pltpu.VMEM((slots, nvars, cols, lat), bf16),
        pltpu.VMEM((nvars, cols, lat), bf16),
        pltpu.VMEM(precision.shape, f32),
        pltpu.VMEM(stations.shape, jnp.int32),
        pltpu.SMEM(ancestors.shape, jnp.int32),
        pltpu.SMEM(tempering.shape, f32),
        pltpu.VMEM(w_in.shape, bf16),
        pltpu.VMEM(w_mid.shape, bf16),
        pltpu.VMEM((3, 3) + w_out.shape[:1:-1], bf16),
        pltpu.VMEM((slots, cols + 6, cin, lat), bf16),
        pltpu.VMEM((cols, cin, lat), bf16),
        pltpu.VMEM((slots, cols + 4, hid, lat), bf16),
        pltpu.VMEM((slots, cols + 2, hid, lat), bf16),
        pltpu.VMEM((3 * hid, 3 * cin), bf16),
        pltpu.VMEM((3 * hid, 3 * hid), bf16),
        pltpu.VMEM((3 * cin, 3 * hid), bf16),
        pltpu.VMEM((cols, lat), f32),
        pltpu.VMEM((slots, 8, lat), f32),
        pltpu.SMEM((128,), jnp.int32),
        pltpu.SMEM((4, 128), jnp.int32),
        pltpu.SMEM((128,), jnp.int32),
        pltpu.SMEM((max(n_ens - 1, 1), 128), jnp.int32),
        pltpu.VMEM((8, 128), f32),
        pltpu.VMEM((max(n_lon - 1, 1), 8, 128), f32),
        pltpu.VMEM((4, 8, 128), f32),
    ]
    scratch += [pltpu.VMEM((2 * slots, len(c), rows, lat), bf16) for c in chunks]
    scratch += [pltpu.VMEM((FIXED, len(c) // 2, rows, lat), bf16) for c in chunks]
    scratch += [pltpu.VMEM((2 * slots, len(chunks[0]), rows, lat), bf16)]
    scratch += [pltpu.VMEM((2, FIXED, len(c) // 2, rows, lat), bf16) for c in chunks[1:]]
    scratch += [dma((slots + 8,))] + [dma((3,))] * 2 + [dma((2,))] * 2 + [dma((n,))] * 6
    scratch += [dma((max(n_lon - 1, 1),))] * 2 + [dma((3,))] * 2 + [dma((max(n_ens - 1, 1),))] * 2
    scratch += [pltpu.SemaphoreType.REGULAR] * 2
    return pl.pallas_call(
        functools.partial(main_kernel, n_lon, n_ens, cin, hid, chunks),
        out_shape=(
            jax.ShapeDtypeStruct((slots, cols, nvars, lat), bf16),
            jax.ShapeDtypeStruct((2 * slots - FIXED, (cols - len(chunks[0])) // 2, rows, lat), bf16),
            jax.ShapeDtypeStruct((1 + slots,), jnp.int32),
            jax.ShapeDtypeStruct((slots,), f32),
        ),
        in_specs=[hbm] * 9,
        out_specs=(vmem, vmem, smem, smem),
        scratch_shapes=scratch,
        compiler_params=pltpu.CompilerParams(
            collective_id=0, has_side_effects=True, vmem_limit_bytes=62 << 20
        ),
        name="step",
    )(particles, observed, precision, stations, ancestors, tempering, w_in, w_mid, w_out.transpose(0, 1, 3, 2))


def more_kernel(extra, chunks, info_ref, out_in, spare_ref, out_ref, arrived, x_s, x_r, fwd_s, fwd_r):
    slots = out_in.shape[0]
    nvars = out_in.shape[2]
    dom = lax.axis_index("dom")
    core = lax.rem(dom, 2)
    sibling, partner = {"dom": dom + 1 - 2 * core}, {"dom": lax.rem(dom + 2, 4)}
    barrier = pltpu.get_barrier_semaphore()
    for peer in (sibling, partner):
        pl.semaphore_signal(barrier, inc=1, device_id=peer, device_id_type=MESH)
    pl.semaphore_wait(barrier, 2)
    spans, at = [], 0
    for chunk in chunks[1:]:
        spans.append((at, len(chunk) // 2))
        at += len(chunk) // 2
    crossings = []
    for j in range(extra):
        for c, (lo, size) in enumerate(spans):
            i = j * len(spans) + c
            crossings.append(remote(
                spare_ref.at[j, pl.ds(lo, size)], arrived.at[core, j, pl.ds(lo, size)],
                x_s.at[i], x_r.at[i], partner,
            ))
    forwards = []
    for j in range(extra):
        for c, (lo, size) in enumerate(spans):
            i = j * len(spans) + c
            crossings[i].wait()
            piece = arrived.at[core, j, pl.ds(lo, size)]
            forwards.append(remote(piece, piece, fwd_s.at[i], fwd_r.at[i], sibling))
    for copy in forwards:
        copy.wait()
    for s in range(slots):
        src = info_ref[1 + s]
        far = jnp.clip(src - (2 * slots + FIXED), 0, extra - 1)
        for x in chunks[0]:
            out_ref[s, x] = out_in[s, x]
        for chunk, (lo, size) in zip(chunks[1:], spans):
            for at, x in enumerate(chunk):
                out_ref[s, x] = jnp.where(
                    src < 2 * slots + FIXED, out_in[s, x], arrived[at // size, far, lo + at % size][:nvars]
                )


def more_call(extra, info, out, spare):
    slots, cols, nvars, lat = out.shape
    chunks = column_chunks(cols)
    vmem = pl.BlockSpec(memory_space=pltpu.VMEM)
    dma = pltpu.SemaphoreType.DMA
    return pl.pallas_call(
        functools.partial(more_kernel, extra, chunks),
        out_shape=jax.ShapeDtypeStruct(out.shape, out.dtype),
        in_specs=[pl.BlockSpec(memory_space=pltpu.SMEM), vmem, vmem],
        out_specs=vmem,
        scratch_shapes=[pltpu.VMEM((2, extra) + spare.shape[1:], out.dtype)] + [dma((extra * len(chunks),))] * 4,
        compiler_params=pltpu.CompilerParams(
            collective_id=extra, has_side_effects=True, vmem_limit_bytes=24 << 20
        ),
        name="more",
    )(info, out, spare)


def two_chips(*args):
    out, spare, info, weights = main_call(*args)
    slots = out.shape[0]
    branches = [lambda info, out, spare: out]
    for extra in range(1, 2 * slots - FIXED + 1):
        branches.append(functools.partial(more_call, extra))
    out = lax.switch(info[0], branches, info, out, spare)
    return (out.transpose(0, 2, 1, 3), weights)


def on_device(*args):
    if lax.axis_size("dom") == 4 and args[0].shape[2] >= 16:
        return two_chips(*args)
    return many_chips(*args)


def solution(mesh):
    return jax.shard_map(
        on_device,
        mesh=mesh,
        in_specs=(
            P(("ens", "dom"), None, "lon", None),
            P("ens", "lon", None),
            P(("ens", "lon"), None),
            P(("ens", "lon"), None),
            P(("ens", "dom")),
            P("ens"),
            P(),
            P(),
            P(),
        ),
        out_specs=(P(("ens", "dom"), None, "lon", None), P(("ens", "dom"))),
        check_vma=False,
    )
```

```python
import functools

import jax
import jax.numpy as jnp
from jax import lax
from jax.experimental import pallas as pl
from jax.experimental.pallas import tpu as pltpu
from jax.sharding import PartitionSpec as P


def pad_to(count, step):
    return -(-count // step) * step


def stacked_taps(weight, out_rows, in_rows):
    _, _, outs, ins = weight.shape
    w = jnp.pad(weight, ((0, 0), (0, 0), (0, out_rows - outs), (0, in_rows - ins)))
    return w.transpose(1, 2, 0, 3).reshape(3 * out_rows, 3 * in_rows)


def conv_column(src_ref, w, x, in_rows, out_rows, first, last):
    window = src_ref[x * in_rows : (x + 3) * in_rows, :]
    p = jnp.dot(w, window, preferred_element_type=jnp.float32)
    lat = p.shape[1]
    below = pltpu.roll(p[:out_rows], 1, 1)
    above = pltpu.roll(p[2 * out_rows :], lat - 1, 1)
    return (
        p[out_rows : 2 * out_rows]
        + jnp.where(first, 0.0, below)
        + jnp.where(last, 0.0, above)
    )


def silu(v):
    half = 0.5 * v
    return half + half * jnp.tanh(half)


def step_kernel(spans, cin, hid, edges, *refs):
    if edges:
        low_ref, high_ref, *refs = refs
    mid_ref, obs_ref, ow_ref, w1_ref, w2_ref, w3_ref, out_ref, ext, a1, a2 = refs
    cols, nvars, lat = mid_ref.shape[1:]
    lane_h = lax.broadcasted_iota(jnp.int32, (hid, lat), 1)
    lane_o = lax.broadcasted_iota(jnp.int32, (cin, lat), 1)
    first_h, last_h = lane_h == 0, lane_h == lat - 1
    first_o, last_o = lane_o == 0, lane_o == lat - 1

    @pl.when(pl.program_id(0) == 0)
    def _():
        ext[...] = jnp.zeros_like(ext)

    at = 0
    for s, (lo, hi) in enumerate(spans):
        for k, x in enumerate(range(lo - 3, hi + 3)):
            if x < 0:
                column = low_ref[0, x + 3]
            elif x >= cols:
                column = high_ref[0, x - cols]
            else:
                column = mid_ref[0, x]
            ext[s, k * cin : k * cin + nvars, :] = column
        for x in range(hi - lo + 4):
            v = conv_column(ext.at[s], w1_ref[...], x, cin, hid, first_h, last_h)
            a1[s, x * hid : (x + 1) * hid, :] = silu(v).astype(jnp.bfloat16)
        for x in range(hi - lo + 2):
            v = conv_column(a1.at[s], w2_ref[...], x, hid, hid, first_h, last_h)
            a2[s, x * hid : (x + 1) * hid, :] = silu(v).astype(jnp.bfloat16)
        for x in range(hi - lo):
            noise = conv_column(a2.at[s], w3_ref[...], x, hid, cin, first_o, last_o)[:nvars]
            current = ext[s, (x + 3) * cin : (x + 4) * cin, :].astype(jnp.float32)[:nvars]
            seen = obs_ref[lo + x].astype(jnp.float32)
            gain = 0.25 * ow_ref[lo + x]
            new = current - 0.5 * noise + gain * (seen - current)
            out_ref[0, at] = new.astype(jnp.bfloat16)
            at += 1


def update_chunk(spans, edges, mid, observed, obs_weight, w1, w2, w3, cin, hid):
    slots, _, nvars, lat = mid.shape
    step = sum(hi - lo for lo, hi in spans)
    widest = max(hi - lo for lo, hi in spans)
    whole = lambda a: pl.BlockSpec(a.shape, lambda p: (0,) * a.ndim)
    own = lambda a: pl.BlockSpec((1,) + a.shape[1:], lambda p: (p, 0, 0, 0))
    return pl.pallas_call(
        functools.partial(step_kernel, spans, cin, hid, bool(edges)),
        out_shape=jax.ShapeDtypeStruct((slots, step, nvars, lat), jnp.bfloat16),
        grid=(slots,),
        in_specs=[own(a) for a in (*edges, mid)]
        + [whole(a) for a in (observed, obs_weight, w1, w2, w3)],
        out_specs=pl.BlockSpec((1, step, nvars, lat), lambda p: (p, 0, 0, 0)),
        scratch_shapes=[
            pltpu.VMEM((len(spans), (widest + 6) * cin, lat), jnp.bfloat16),
            pltpu.VMEM((len(spans), (widest + 4) * hid, lat), jnp.bfloat16),
            pltpu.VMEM((len(spans), (widest + 2) * hid, lat), jnp.bfloat16),
        ],
        compiler_params=pltpu.CompilerParams(vmem_limit_bytes=56 << 20),
        cost_estimate=pl.CostEstimate(flops=0, bytes_accessed=1024, transcendentals=0),
        name="update_chunk",
    )(*edges, mid, observed, obs_weight, w1, w2, w3)


def exchange_kernel(n_lon, mid_ref, sums_ref, low_ref, high_ref, total_ref, parts, edge_send, edge_recv, lon_send, lon_recv):
    lon = lax.axis_index("lon")
    cols = mid_ref.shape[1]

    def lon_at(k):
        return {"lon": lax.rem(lon + k, n_lon)}

    barrier = pltpu.get_barrier_semaphore()
    for k in range(1, n_lon):
        pl.semaphore_signal(barrier, inc=1, device_id=lon_at(k), device_id_type=pl.DeviceIdType.MESH)
    pl.semaphore_wait(barrier, n_lon - 1)

    def send(src, dst, s, r, target):
        copy = pltpu.make_async_remote_copy(
            src_ref=src, dst_ref=dst, send_sem=s, recv_sem=r,
            device_id=target, device_id_type=pl.DeviceIdType.MESH,
        )
        copy.start()
        return copy

    edges = [
        send(mid_ref.at[:, cols - 3 : cols], low_ref, edge_send.at[0], edge_recv.at[0], lon_at(1)),
        send(mid_ref.at[:, 0:3], high_ref, edge_send.at[1], edge_recv.at[1], lon_at(n_lon - 1)),
    ]
    parts[lon] = sums_ref[...]
    over_lon = [
        send(sums_ref, parts.at[lon], lon_send.at[k - 1], lon_recv.at[k - 1], lon_at(k))
        for k in range(1, n_lon)
    ]
    for copy in over_lon:
        copy.wait()
    band_sum = parts[0]
    for k in range(1, n_lon):
        band_sum = band_sum + parts[k]
    total_ref[...] = band_sum
    for copy in edges:
        copy.wait()


def exchange(mid, sums, n_lon):
    slots, _, nvars, lat = mid.shape
    edge = jax.ShapeDtypeStruct((slots, 3, nvars, lat), mid.dtype)
    vmem = pl.BlockSpec(memory_space=pltpu.VMEM)
    return pl.pallas_call(
        functools.partial(exchange_kernel, n_lon),
        out_shape=(edge, edge, jax.ShapeDtypeStruct(sums.shape, jnp.float32)),
        in_specs=[pl.BlockSpec(memory_space=pl.ANY), vmem],
        out_specs=(vmem, vmem, vmem),
        scratch_shapes=[
            pltpu.VMEM((n_lon,) + sums.shape, jnp.float32),
            pltpu.SemaphoreType.DMA((2,)),
            pltpu.SemaphoreType.DMA((2,)),
            pltpu.SemaphoreType.DMA((n_lon - 1,)),
            pltpu.SemaphoreType.DMA((n_lon - 1,)),
        ],
        compiler_params=pltpu.CompilerParams(collective_id=0, has_side_effects=True),
        cost_estimate=pl.CostEstimate(flops=0, bytes_accessed=1024, transcendentals=0),
        name="exchange",
    )(mid, sums)


def across(u):
    n = lax.axis_size("dom")
    return [u] + [
        lax.ppermute(u, "dom", [(d, (d + 2 * k) % n) for d in range(n)]) for k in range(1, n // 2)
    ]


def pick_kernel(slots, base, codes_ref, *refs):
    *pieces, out_ref = refs
    if base == 0:
        received_ref, *pieces = pieces
    for s in range(slots):
        for m in range(len(pieces) * slots):
            wanted = codes_ref[base + s] == m
            if base == 0:
                wanted = wanted & (codes_ref[2 * slots + s] == 1)

            @pl.when(wanted)
            def _():
                out_ref[s] = pieces[m // slots][m % slots]

        if base == 0:

            @pl.when(codes_ref[2 * slots + s] == 0)
            def _():
                out_ref[s] = received_ref[s]


def pick(codes, base, arrays):
    u = arrays[0]
    slots = u.shape[0]
    vmem = pl.BlockSpec(memory_space=pltpu.VMEM)
    return pl.pallas_call(
        functools.partial(pick_kernel, slots, base),
        out_shape=jax.ShapeDtypeStruct(u.shape, u.dtype),
        in_specs=[pl.BlockSpec(memory_space=pltpu.SMEM)] + [vmem] * len(arrays),
        out_specs=vmem,
        compiler_params=pltpu.CompilerParams(vmem_limit_bytes=24 << 20),
        cost_estimate=pl.CostEstimate(flops=0, bytes_accessed=1024, transcendentals=0),
        name="pick",
    )(codes, *arrays)


def weight_kernel(slots, t_ref, *refs):
    *part_refs, out_ref = refs
    shape = out_ref.shape
    real = lax.broadcasted_iota(jnp.int32, shape, 0) < slots
    count = len(part_refs) * slots

    def over_particles(rows):
        total = rows[0]
        for row in rows[1:]:
            total = total + row
        return jnp.sum(total, axis=0, keepdims=True)

    misfits = [jnp.broadcast_to(jnp.sum(r[...], axis=1, keepdims=True), shape) for r in part_refs]
    center = over_particles([jnp.where(real, m, 0.0) for m in misfits]) / count
    deviations = [jnp.where(real, m - center, 0.0) for m in misfits]
    spread = jnp.sqrt(over_particles([d * d for d in deviations]) / count + 1.0)
    expos = [jnp.where(real, jnp.exp(-0.5 * t_ref[0] * d / spread), 0.0) for d in deviations]
    out_ref[...] = expos[0] / over_particles(expos)


def own_weights_of(parts, tempering, slots):
    vmem = pl.BlockSpec(memory_space=pltpu.VMEM)
    out = pl.pallas_call(
        functools.partial(weight_kernel, slots),
        out_shape=jax.ShapeDtypeStruct(parts[0].shape, jnp.float32),
        in_specs=[pl.BlockSpec(memory_space=pltpu.SMEM)] + [vmem] * len(parts),
        out_specs=vmem,
        name="own_weights",
    )(tempering, *parts)
    return out[:slots, 0]


def many_chips(particles, observed, precision, stations, ancestors, tempering, w_in, w_mid, w_out):
    slots, nvars, cols, lat = particles.shape
    hid = w_mid.shape[2]
    cin = pad_to(nvars, 16)
    n_dom, n_lon = lax.axis_size("dom"), lax.axis_size("lon")
    me = lax.axis_index("dom")
    mid = particles.transpose(0, 2, 1, 3)
    sibling_anc = lax.ppermute(ancestors, "dom", [(d, d ^ 1) for d in range(n_dom)])

    obs_weight = stations.astype(jnp.float32) * precision
    wanted = jnp.concatenate([ancestors, sibling_anc])
    owner = lax.div(wanted, slots)
    chips = n_dom // 2
    steps = lax.rem(lax.shift_right_logical(me, 1) - lax.div(owner, 2) + chips, chips)
    candidate = steps * slots + lax.rem(wanted, slots)
    here = lax.rem(owner, 2) == (me & 1)

    obs_columns = observed.transpose(1, 0, 2)
    ow_columns = obs_weight[:, None, :]
    w1 = stacked_taps(w_in, hid, cin)
    w2 = stacked_taps(w_mid, hid, hid)
    w3 = stacked_taps(w_out, cin, hid)

    update = lambda spans, edges: update_chunk(
        spans, edges, mid, obs_columns, ow_columns, w1, w2, w3, cin, hid
    )
    u = update([(3, cols - 3)], [])
    groups = [across(u)]

    late_weight, _ = lax.optimization_barrier((obs_weight, u))
    misfit_cell = particles.astype(jnp.float32) - observed.astype(jnp.float32)[None]
    local_sums = jnp.sum(late_weight[None, None] * misfit_cell * misfit_cell, axis=(1, 2))
    sums = jnp.sum(local_sums.reshape(slots, lat // 128, 128), axis=1)
    sums = jnp.pad(sums, ((0, pad_to(slots, 8) - slots), (0, 0)))
    low, high, band_sums = exchange(mid, sums, n_lon)
    groups.append(across(update([(0, 3), (cols - 3, cols)], [low, high])))

    parts = [band_sums] + [
        lax.ppermute(band_sums, "dom", [(d, (d + k) % n_dom) for d in range(n_dom)])
        for k in range(1, n_dom)
    ]
    own_weights = own_weights_of(parts, tempering, slots)

    codes = jnp.concatenate([candidate, here[:slots].astype(jnp.int32)])
    groups = lax.optimization_barrier(groups)
    results = []
    for pieces in groups:
        sent = pick(codes, slots, pieces)
        received = lax.ppermute(sent, "dom", [(d, d ^ 1) for d in range(n_dom)])
        results.append(pick(codes, 0, [received, *pieces]))
    inner, sides = results
    new_columns = jnp.concatenate([sides[:, :3], inner, sides[:, 3:]], axis=1)
    return (new_columns.transpose(0, 2, 1, 3), own_weights)


MESH = pl.DeviceIdType.MESH
FIXED = 2


def column_chunks(cols):
    middle = cols // 2
    chunks = [[middle - 1, middle]]
    above, below = list(range(middle + 1, cols - 3)), list(range(3, middle - 1))
    for side, take in ((above, lambda v, k: v[:k]), (below, lambda v, k: v[-k:])):
        left = side
        while left:
            size = 4 if len(left) >= 6 or len(left) == 4 else min(len(left), 6)
            part = take(left, size)
            chunks.append(part)
            left = [x for x in left if x not in part]
    return chunks


def remote(src, dst, s, r, target):
    copy = pltpu.make_async_remote_copy(
        src_ref=src, dst_ref=dst, send_sem=s, recv_sem=r, device_id=target, device_id_type=MESH
    )
    copy.start()
    return copy


def main_kernel(n_lon, n_ens, cin, hid, chunks, *refs):
    (part_hbm, obs_hbm, prec_hbm, stat_hbm, anc_hbm, temp_hbm, win_hbm, wmid_hbm, wout_hbm,
     out_ref, spare_ref, info_ref, wts_ref,
     raw, raw_obs, prec_ref, stat_ref, anc_ref, temp_ref, win_ref, wmid_ref, wout_ref, ext, obs_cm, a1, a2, w1, w2, w3, gain, misfit, anc_own, anc_all, k_own, k_all,
     lon_sum, lon_parts, dom_parts, *rest) = refs
    inner = len(chunks)
    n = inner + 2
    mine, gathered, arrived = rest[:n], rest[n : 2 * n], rest[2 * n : 3 * n]
    (load_sem, anc_s, anc_r, halo_s, halo_r, sib_s, sib_r, x_s, x_r, fwd_s, fwd_r,
     lon_s, lon_r, dom_s, dom_r, ens_s, ens_r, from_low, from_high) = rest[3 * n :]
    slots, nvars, cols, lat = part_hbm.shape
    rows = spare_ref.shape[2]
    f32, bf16 = jnp.float32, jnp.bfloat16

    dom, lon, ens = lax.axis_index("dom"), lax.axis_index("lon"), lax.axis_index("ens")
    core, chip = lax.rem(dom, 2), lax.div(dom, 2)
    sibling, partner = {"dom": dom + 1 - 2 * core}, {"dom": lax.rem(dom + 2, 4)}

    def lon_at(k):
        return {"lon": lax.rem(lon + k, n_lon)}

    def dom_at(k):
        return {"dom": lax.rem(dom + k, 4)}

    def ens_at(k):
        return {"ens": lax.rem(ens + k, n_ens)}

    peers = [dom_at(k) for k in range(1, 4)] + [ens_at(k) for k in range(1, n_ens)]
    barrier = pltpu.get_barrier_semaphore()
    for peer in peers:
        pl.semaphore_signal(barrier, inc=1, device_id=peer, device_id_type=MESH)

    @pl.when(lon < n_lon - 1)
    def _():
        pl.semaphore_signal(barrier, inc=1, device_id=lon_at(1), device_id_type=MESH)

    @pl.when(lon > 0)
    def _():
        pl.semaphore_signal(barrier, inc=1, device_id=lon_at(n_lon - 1), device_id_type=MESH)

    def load(src, dst, i):
        copy = pltpu.make_async_copy(src, dst, load_sem.at[i])
        copy.start()
        return copy

    names = [
        (anc_hbm, anc_ref), (win_hbm, win_ref), (wmid_hbm, wmid_ref), (wout_hbm, wout_ref),
        (prec_hbm, prec_ref), (stat_hbm, stat_ref), (temp_hbm, temp_ref),
    ]
    small = [load(src, dst, slots + 1 + i) for i, (src, dst) in enumerate(names)]
    states = [load(part_hbm.at[p], raw.at[p], p) for p in range(slots)]
    seen = load(obs_hbm, raw_obs, slots)

    w1[...] = jnp.zeros_like(w1)
    w3[...] = jnp.zeros_like(w3)
    misfit[...] = jnp.zeros_like(misfit)
    small[0].wait()
    for s in range(slots):
        anc_own[s] = anc_ref[s]
        anc_all[dom, s] = anc_ref[s]

    @pl.when((lon > 0) & (lon < n_lon - 1))
    def _():
        pl.semaphore_wait(barrier, len(peers) + 2)

    @pl.when((lon == 0) | (lon == n_lon - 1))
    def _():
        pl.semaphore_wait(barrier, len(peers) + 1)

    sent_anc = [
        remote(anc_own, anc_all.at[dom], anc_s.at[k - 1], anc_r.at[k - 1], dom_at(k))
        for k in range(1, 4)
    ]
    @pl.when(lon == 0)
    def _():
        pl.semaphore_signal(from_low, inc=1, device_id=lon_at(1), device_id_type=MESH)

    @pl.when(lon == n_lon - 1)
    def _():
        pl.semaphore_signal(from_high, inc=1, device_id=lon_at(n_lon - 1), device_id_type=MESH)

    def relay(r):
        @pl.when(lon == r)
        def _():
            pl.semaphore_wait(from_low, 1)
            if r < n_lon - 1:
                pl.semaphore_signal(from_low, inc=1, device_id=lon_at(1), device_id_type=MESH)

        @pl.when(lon == n_lon - 1 - r)
        def _():
            pl.semaphore_wait(from_high, 1)
            if r < n_lon - 1:
                pl.semaphore_signal(from_high, inc=1, device_id=lon_at(n_lon - 1), device_id_type=MESH)

    def turn(src, dst, at, x0):
        width = 8
        for q in range(0, cin, 16):
            count = min(16, nvars - q)
            v = src[q : q + count, x0 : x0 + width, :].astype(f32)
            if count < 16:
                v = jnp.concatenate([v, jnp.zeros((16 - count, width, lat), f32)], axis=0)
            dst[at + x0 : at + x0 + width, q : q + 16, :] = jnp.swapaxes(v, 0, 1).astype(bf16)

    middle = 8 * (cols // 16)
    outer = [x0 for x0 in range(0, cols, 8) if x0 != middle]
    for p in range(slots):
        states[p].wait()
        for x0 in outer:
            turn(raw.at[p], ext.at[p], 3, x0)

    def edge(up, start):
        if up:
            src, dst, k, target = ext.at[:, cols : cols + 3], ext.at[:, 0:3], 0, lon_at(1)
        else:
            src, dst, k, target = ext.at[:, 3:6], ext.at[:, cols + 3 : cols + 6], 1, lon_at(n_lon - 1)
        copy = pltpu.make_async_remote_copy(
            src_ref=src, dst_ref=dst, send_sem=halo_s.at[k], recv_sem=halo_r.at[k],
            device_id=target, device_id_type=MESH,
        )
        if start:
            copy.start()
        return copy

    @pl.when(lon < n_lon - 1)
    def _():
        edge(True, True)

    @pl.when(lon > 0)
    def _():
        edge(False, True)

    relay(1)
    for copy in small[1:]:
        copy.wait()
    for j in range(3):
        for i in range(3):
            w1[j * hid : (j + 1) * hid, i * cin : i * cin + nvars] = win_ref[i, j]
            w2[j * hid : (j + 1) * hid, i * hid : (i + 1) * hid] = wmid_ref[i, j]
            turned = wout_ref[i, j].astype(f32).T
            w3[j * cin : j * cin + nvars, i * hid : (i + 1) * hid] = turned.astype(bf16)
    gain[...] = 0.25 * (stat_ref[...].astype(f32) * prec_ref[...])

    relay(2)
    for p in range(slots):
        turn(raw.at[p], ext.at[p], 3, middle)
    seen.wait()
    turn(raw_obs, obs_cm, 0, middle)

    lane_h = lax.broadcasted_iota(jnp.int32, (hid, lat), 1)
    lane_o = lax.broadcasted_iota(jnp.int32, (cin, lat), 1)
    edges_h = (lane_h == 0, lane_h == lat - 1)
    edges_o = (lane_o == 0, lane_o == lat - 1)

    def conv(src, w, x, out_rows, edges):
        window = src[pl.ds(x, 3)]
        window = window.reshape(window.shape[0] * window.shape[1], lat)
        v = jnp.dot(w[...], window, preferred_element_type=f32)
        below = pltpu.roll(v[:out_rows], 1, 1)
        above = pltpu.roll(v[2 * out_rows :], lat - 1, 1)
        return (
            v[out_rows : 2 * out_rows]
            + jnp.where(edges[0], 0.0, below)
            + jnp.where(edges[1], 0.0, above)
        )

    def first(p, x):
        a1[p, x + 2] = silu(conv(ext.at[p], w1, x + 2, hid, edges_h)).astype(bf16)

    def second(p, x):
        a2[p, x + 1] = silu(conv(a1.at[p], w2, x + 1, hid, edges_h)).astype(bf16)

    def third(p, x, dst, at):
        noise = conv(a2.at[p], w3, x, cin, edges_o)
        current = ext[p, x + 3].astype(f32)
        diff = obs_cm[x].astype(f32) - current
        pull = gain[pl.ds(x, 1), :] * diff
        new = current - 0.5 * noise + pull
        dst[p, at] = new[:rows].astype(bf16)
        square = pull * diff
        total = square[0:8]
        for r in range(8, cin, 8):
            total = total + square[r : r + 8]
        misfit[p] += total

    def share(c):
        return remote(mine[c].at[0:slots], mine[c].at[slots : 2 * slots], sib_s.at[c], sib_r.at[c], sibling)

    def choose():
        theirs = [anc_all[2 * (1 - chip) + i, s] for i in range(2) for s in range(slots)]
        ours = [anc_all[2 * chip + i, s] for i in range(2) for s in range(slots)]
        group = 2 * slots
        one, zero = jnp.int32(1), jnp.int32(0)

        def wanted(ids, base):
            flags = []
            for r in range(group):
                flag = zero
                for g in ids:
                    flag = jnp.where(g == base + r, one, flag)
                flags.append(flag)
            return flags

        give = wanted(theirs, group * chip)
        take = wanted(ours, group * (1 - chip))
        order, count = [zero] * group, zero
        for r in range(group):
            for j in range(r + 1):
                order[j] = jnp.where((count == j) & (give[r] == 1), jnp.int32(r), order[j])
            count = count + give[r]
        near = [jnp.where(lax.div(r, slots) == core, zero, jnp.int32(slots)) + lax.rem(r, slots) for r in order]
        ranks, got = [], zero
        for r in range(group):
            ranks.append(got)
            got = got + take[r]
        sources, remotes = [], []
        for s in range(slots):
            g = anc_ref[s]
            r = g - group * lax.div(g, group)
            rank = zero
            for m in range(group):
                rank = jnp.where(r == m, ranks[m], rank)
            local = jnp.where(lax.div(r, slots) == core, zero, jnp.int32(slots)) + lax.rem(r, slots)
            sources.append(jnp.where(lax.div(g, group) == chip, local, group + rank))
            remotes.append(r)
        return near, sources, remotes, jnp.maximum(count, got)

    state = {}

    def pass_on(c, shared):
        shared.wait()
        if c >= inner:
            chosen = jnp.where(core == 0, state["near"][0], state["near"][1])
            for t in range(3):
                gathered[c][t] = mine[c][chosen, t]
            base = sum(len(chunk) for chunk in chunks[1:]) // 2
            if c == n - 1:
                for j in range(FIXED, 2 * slots):
                    for t in range(3):
                        spare_ref[j - FIXED, base + t] = jnp.where(
                            core == 0, mine[inner][state["near"][j], t], mine[c][state["near"][j], t]
                        )
            return remote(gathered[c], arrived[c].at[core], x_s.at[c], x_r.at[c], partner)
        half = len(chunks[c]) // 2
        start = core * half
        for j in range(FIXED):
            for t in range(half):
                gathered[c][j, t] = mine[c][state["near"][j], start + t]
        base = sum(len(chunk) for chunk in chunks[1:c]) // 2
        for j in range(FIXED, 2 * slots):
            for t in range(half):
                spare_ref[j - FIXED, base + t] = mine[c][state["near"][j], start + t]
        return remote(gathered[c], arrived[c].at[core], x_s.at[c], x_r.at[c], partner)

    ready = [set(), set()]

    def compute(c):
        one = sorted({x + d for x in chunks[c] for d in range(-2, 3)} - ready[0])
        two = sorted({x + d for x in chunks[c] for d in range(-1, 2)} - ready[1])
        ready[0].update(one)
        ready[1].update(two)
        for x in one:
            for p in range(slots):
                first(p, x)
        for x in two:
            for p in range(slots):
                second(p, x)
        for at, x in enumerate(chunks[c]):
            for p in range(slots):
                third(p, x, mine[c], at)

    first_side = jnp.where(lon == 0, 1, 0)
    sides = {inner: first_side, inner + 1: 1 - first_side}

    def compute_edge(c):
        side = sides[c]
        for t in range(3):
            for p in range(slots):
                first(p, side * (cols + 1) - 2 + t)
        for t in range(3):
            for p in range(slots):
                second(p, side * (cols - 1) - 1 + t)
        for t in range(3):
            for p in range(slots):
                third(p, side * (cols - 3) + t, mine[c], t)

    compute(0)
    ends = pl.ds(core * slots, slots)
    crossings = [
        remote(mine[0].at[0:slots], arrived[0].at[ends], x_s.at[0], x_r.at[0], partner)
    ]

    shares = [share(0)]
    for r in range(3, n_lon):
        relay(r)

    @pl.when(lon == n_lon - 1)
    def _():
        edge(True, True)

    @pl.when(lon == 0)
    def _():
        edge(False, True)

    for x0 in outer:
        turn(raw_obs, obs_cm, 0, x0)
    compute(1)
    shares.append(share(1))
    for copy in sent_anc:
        copy.wait()
    near, sources, remotes, most = choose()
    k_own[0] = most
    state["near"], state["sources"], state["remotes"] = near, sources, remotes
    state["ens"] = [
        remote(k_own, k_all.at[k - 1], ens_s.at[k - 1], ens_r.at[k - 1], ens_at(k))
        for k in range(1, n_ens)
    ]
    shares[0].wait()
    crossings.append(pass_on(1, shares[1]))
    compute(2)
    shares.append(share(2))
    crossings.append(pass_on(2, shares[2]))
    for c in range(3, inner):
        compute(c)
        shares.append(share(c))
        if c > 3:
            crossings.append(pass_on(c - 1, shares[c - 1]))
    for c in (inner, inner + 1):
        @pl.when(sides[c] == 0)
        def _():
            edge(True, False).wait_recv()

        @pl.when(sides[c] == 1)
        def _():
            edge(False, False).wait_recv()

        compute_edge(c)
        shares.append(share(c))
        if c == inner:
            crossings.append(pass_on(c - 1, shares[c - 1]))
        crossings.append(pass_on(c, shares[c]))
    edge(True, False).wait_send()
    edge(False, False).wait_send()

    sums = [jnp.sum(misfit[p], axis=0, keepdims=True) for p in range(slots)]
    sums = [s[:, :128] + s[:, 128:] for s in sums]
    row = lax.broadcasted_iota(jnp.int32, (8, 128), 0)
    local = jnp.zeros((8, 128), f32)
    for p in range(slots):
        local = jnp.where(row == p, sums[p], local)
    lon_sum[...] = 4.0 * local
    sent = [
        remote(lon_sum, lon_parts.at[k - 1], lon_s.at[k - 1], lon_r.at[k - 1], lon_at(k))
        for k in range(1, n_lon)
    ]
    forwards = []

    def finish(c):
        forwards[c].wait()
        half = len(chunks[c]) // 2 if c < inner else 0
        for s in range(slots):
            src = state["sources"][s]
            near = jnp.minimum(src, 2 * slots - 1)
            far = jnp.clip(src - 2 * slots, 0, FIXED - 1)
            if c >= inner:
                for at in range(3):
                    out_ref[s, sides[c] * (cols - 3) + at] = jnp.where(
                        src < 2 * slots, mine[c][near, at], arrived[c][far, at]
                    )[:nvars]
                continue
            for at, x in enumerate(chunks[c]):
                if c == 0:
                    far_away = arrived[c][state["remotes"][s], at]
                else:
                    far_away = arrived[c][at // half, far, at % half]
                out_ref[s, x] = jnp.where(src < 2 * slots, mine[c][near, at], far_away)[:nvars]

    for c in range(n):
        crossings[c].wait()
        piece = arrived[c].at[ends if c == 0 else core]
        forwards.append(remote(piece, piece, fwd_s.at[c], fwd_r.at[c], sibling))
        if c == n - 3:
            for copy in sent:
                copy.wait()
            band = lon_sum[...]
            for k in range(1, n_lon):
                band = band + lon_parts[k - 1]
            dom_parts[0] = band
            sent = [
                remote(dom_parts.at[0], dom_parts.at[k], dom_s.at[k - 1], dom_r.at[k - 1], dom_at(k))
                for k in range(1, 4)
            ]
        if c == n - 2:
            for copy in sent:
                copy.wait()
            misfits = [jnp.broadcast_to(jnp.sum(dom_parts[k], axis=1, keepdims=True), (8, 128)) for k in range(4)]
            real = row < slots

            def over(values):
                total = values[0]
                for value in values[1:]:
                    total = total + value
                return jnp.sum(jnp.where(real, total, 0.0), axis=0, keepdims=True)

            center = over(misfits) / (4 * slots)
            off = [m - center for m in misfits]
            spread = jnp.sqrt(over([d * d for d in off]) / (4 * slots) + 1.0)
            expos = [jnp.exp(-0.5 * temp_ref[0] * d / spread) for d in off]
            own = expos[0] / over(expos)
            lane = lax.broadcasted_iota(jnp.int32, (8, 128), 1)
            for s in range(slots):
                wts_ref[s] = jnp.sum(jnp.where((row == s) & (lane == 0), own, 0.0))
        if c > 0:
            finish(c - 1)
    finish(n - 1)

    most = k_own[0]
    for copy in state["ens"]:
        copy.wait()
    for k in range(1, n_ens):
        most = jnp.maximum(most, k_all[k - 1, 0])
    info_ref[0] = jnp.maximum(most - FIXED, 0)
    for s in range(slots):
        info_ref[1 + s] = state["sources"][s]


def main_call(particles, observed, precision, stations, ancestors, tempering, w_in, w_mid, w_out):
    slots, nvars, cols, lat = particles.shape
    hid = w_mid.shape[2]
    cin, rows = pad_to(nvars, 16), pad_to(nvars, 8)
    n_lon, n_ens = lax.axis_size("lon"), lax.axis_size("ens")
    chunks = column_chunks(cols)
    n = len(chunks) + 2
    bf16, f32 = jnp.bfloat16, jnp.float32
    vmem = pl.BlockSpec(memory_space=pltpu.VMEM)
    smem = pl.BlockSpec(memory_space=pltpu.SMEM)
    hbm = pl.BlockSpec(memory_space=pltpu.HBM)
    dma = pltpu.SemaphoreType.DMA
    scratch = [
        pltpu.VMEM((slots, nvars, cols, lat), bf16),
        pltpu.VMEM((nvars, cols, lat), bf16),
        pltpu.VMEM(precision.shape, f32),
        pltpu.VMEM(stations.shape, jnp.int32),
        pltpu.SMEM(ancestors.shape, jnp.int32),
        pltpu.SMEM(tempering.shape, f32),
        pltpu.VMEM(w_in.shape, bf16),
        pltpu.VMEM(w_mid.shape, bf16),
        pltpu.VMEM((3, 3) + w_out.shape[:1:-1], bf16),
        pltpu.VMEM((slots, cols + 6, cin, lat), bf16),
        pltpu.VMEM((cols, cin, lat), bf16),
        pltpu.VMEM((slots, cols + 4, hid, lat), bf16),
        pltpu.VMEM((slots, cols + 2, hid, lat), bf16),
        pltpu.VMEM((3 * hid, 3 * cin), bf16),
        pltpu.VMEM((3 * hid, 3 * hid), bf16),
        pltpu.VMEM((3 * cin, 3 * hid), bf16),
        pltpu.VMEM((cols, lat), f32),
        pltpu.VMEM((slots, 8, lat), f32),
        pltpu.SMEM((128,), jnp.int32),
        pltpu.SMEM((4, 128), jnp.int32),
        pltpu.SMEM((128,), jnp.int32),
        pltpu.SMEM((max(n_ens - 1, 1), 128), jnp.int32),
        pltpu.VMEM((8, 128), f32),
        pltpu.VMEM((max(n_lon - 1, 1), 8, 128), f32),
        pltpu.VMEM((4, 8, 128), f32),
    ]
    scratch += [pltpu.VMEM((2 * slots, len(c), rows, lat), bf16) for c in chunks]
    scratch += [pltpu.VMEM((2 * slots, 3, rows, lat), bf16)] * 2
    scratch += [pltpu.VMEM((FIXED, len(c) // 2, rows, lat), bf16) for c in chunks]
    scratch += [pltpu.VMEM((3, rows, lat), bf16)] * 2
    scratch += [pltpu.VMEM((2 * slots, len(chunks[0]), rows, lat), bf16)]
    scratch += [pltpu.VMEM((2, FIXED, len(c) // 2, rows, lat), bf16) for c in chunks[1:]]
    scratch += [pltpu.VMEM((2, 3, rows, lat), bf16)] * 2
    scratch += [dma((slots + 8,))] + [dma((3,))] * 2 + [dma((2,))] * 2 + [dma((n,))] * 6
    scratch += [dma((max(n_lon - 1, 1),))] * 2 + [dma((3,))] * 2 + [dma((max(n_ens - 1, 1),))] * 2
    scratch += [pltpu.SemaphoreType.REGULAR] * 2
    return pl.pallas_call(
        functools.partial(main_kernel, n_lon, n_ens, cin, hid, chunks),
        out_shape=(
            jax.ShapeDtypeStruct((slots, cols, nvars, lat), bf16),
            jax.ShapeDtypeStruct((2 * slots - FIXED, (cols - len(chunks[0])) // 2, rows, lat), bf16),
            jax.ShapeDtypeStruct((1 + slots,), jnp.int32),
            jax.ShapeDtypeStruct((slots,), f32),
        ),
        in_specs=[hbm] * 9,
        out_specs=(vmem, vmem, smem, smem),
        scratch_shapes=scratch,
        compiler_params=pltpu.CompilerParams(
            collective_id=0, has_side_effects=True, vmem_limit_bytes=62 << 20
        ),
        name="step",
    )(particles, observed, precision, stations, ancestors, tempering, w_in, w_mid, w_out.transpose(0, 1, 3, 2))


def more_kernel(extra, chunks, info_ref, out_in, spare_ref, out_ref, arrived, x_s, x_r, fwd_s, fwd_r):
    slots = out_in.shape[0]
    nvars = out_in.shape[2]
    dom = lax.axis_index("dom")
    core = lax.rem(dom, 2)
    sibling, partner = {"dom": dom + 1 - 2 * core}, {"dom": lax.rem(dom + 2, 4)}
    barrier = pltpu.get_barrier_semaphore()
    for peer in (sibling, partner):
        pl.semaphore_signal(barrier, inc=1, device_id=peer, device_id_type=MESH)
    pl.semaphore_wait(barrier, 2)
    cols = out_in.shape[1]
    first_side = jnp.where(lax.axis_index("lon") == 0, 1, 0)
    spans, at = [], 0
    for chunk in chunks[1:]:
        spans.append((at, len(chunk) // 2))
        at += len(chunk) // 2
    spans.append((at, 3))
    crossings = []
    for j in range(extra):
        for c, (lo, size) in enumerate(spans):
            i = j * len(spans) + c
            crossings.append(remote(
                spare_ref.at[j, pl.ds(lo, size)], arrived.at[core, j, pl.ds(lo, size)],
                x_s.at[i], x_r.at[i], partner,
            ))
    forwards = []
    for j in range(extra):
        for c, (lo, size) in enumerate(spans):
            i = j * len(spans) + c
            crossings[i].wait()
            piece = arrived.at[core, j, pl.ds(lo, size)]
            forwards.append(remote(piece, piece, fwd_s.at[i], fwd_r.at[i], sibling))
    for copy in forwards:
        copy.wait()
    for s in range(slots):
        src = info_ref[1 + s]
        far = jnp.clip(src - (2 * slots + FIXED), 0, extra - 1)
        for x in chunks[0]:
            out_ref[s, x] = out_in[s, x]
        for chunk, (lo, size) in zip(chunks[1:], spans):
            for at, x in enumerate(chunk):
                out_ref[s, x] = jnp.where(
                    src < 2 * slots + FIXED, out_in[s, x], arrived[at // size, far, lo + at % size][:nvars]
                )
        lo = spans[-1][0]
        for half, side in enumerate((first_side, 1 - first_side)):
            for t in range(3):
                x = side * (cols - 3) + t
                out_ref[s, x] = jnp.where(
                    src < 2 * slots + FIXED, out_in[s, x], arrived[half, far, lo + t][:nvars]
                )


def more_call(extra, info, out, spare):
    slots, cols, nvars, lat = out.shape
    chunks = column_chunks(cols)
    vmem = pl.BlockSpec(memory_space=pltpu.VMEM)
    dma = pltpu.SemaphoreType.DMA
    return pl.pallas_call(
        functools.partial(more_kernel, extra, chunks),
        out_shape=jax.ShapeDtypeStruct(out.shape, out.dtype),
        in_specs=[pl.BlockSpec(memory_space=pltpu.SMEM), vmem, vmem],
        out_specs=vmem,
        scratch_shapes=[pltpu.VMEM((2, extra) + spare.shape[1:], out.dtype)] + [dma((extra * (len(chunks) + 1),))] * 4,
        compiler_params=pltpu.CompilerParams(
            collective_id=extra, has_side_effects=True, vmem_limit_bytes=24 << 20
        ),
        name="more",
    )(info, out, spare)


def two_chips(*args):
    out, spare, info, weights = main_call(*args)
    slots = out.shape[0]
    branches = [lambda info, out, spare: out]
    for extra in range(1, 2 * slots - FIXED + 1):
        branches.append(functools.partial(more_call, extra))
    out = lax.switch(info[0], branches, info, out, spare)
    return (out.transpose(0, 2, 1, 3), weights)


def on_device(*args):
    if lax.axis_size("dom") == 4 and args[0].shape[2] >= 16:
        return two_chips(*args)
    return many_chips(*args)


def solution(mesh):
    return jax.shard_map(
        on_device,
        mesh=mesh,
        in_specs=(
            P(("ens", "dom"), None, "lon", None),
            P("ens", "lon", None),
            P(("ens", "lon"), None),
            P(("ens", "lon"), None),
            P(("ens", "dom")),
            P("ens"),
            P(),
            P(),
            P(),
        ),
        out_specs=(P(("ens", "dom"), None, "lon", None), P(("ens", "dom"))),
        check_vma=False,
    )
```

```python
import functools

import jax
import jax.numpy as jnp
from jax import lax
from jax.experimental import pallas as pl
from jax.experimental.pallas import tpu as pltpu
from jax.sharding import PartitionSpec as P


def pad_to(count, step):
    return -(-count // step) * step


def stacked_taps(weight, out_rows, in_rows):
    _, _, outs, ins = weight.shape
    w = jnp.pad(weight, ((0, 0), (0, 0), (0, out_rows - outs), (0, in_rows - ins)))
    return w.transpose(1, 2, 0, 3).reshape(3 * out_rows, 3 * in_rows)


def conv_column(src_ref, w, x, in_rows, out_rows, first, last):
    window = src_ref[x * in_rows : (x + 3) * in_rows, :]
    p = jnp.dot(w, window, preferred_element_type=jnp.float32)
    lat = p.shape[1]
    below = pltpu.roll(p[:out_rows], 1, 1)
    above = pltpu.roll(p[2 * out_rows :], lat - 1, 1)
    return (
        p[out_rows : 2 * out_rows]
        + jnp.where(first, 0.0, below)
        + jnp.where(last, 0.0, above)
    )


def silu(v):
    half = 0.5 * v
    return half + half * jnp.tanh(half)


def step_kernel(spans, cin, hid, edges, *refs):
    if edges:
        low_ref, high_ref, *refs = refs
    mid_ref, obs_ref, ow_ref, w1_ref, w2_ref, w3_ref, out_ref, ext, a1, a2 = refs
    cols, nvars, lat = mid_ref.shape[1:]
    lane_h = lax.broadcasted_iota(jnp.int32, (hid, lat), 1)
    lane_o = lax.broadcasted_iota(jnp.int32, (cin, lat), 1)
    first_h, last_h = lane_h == 0, lane_h == lat - 1
    first_o, last_o = lane_o == 0, lane_o == lat - 1

    @pl.when(pl.program_id(0) == 0)
    def _():
        ext[...] = jnp.zeros_like(ext)

    at = 0
    for s, (lo, hi) in enumerate(spans):
        for k, x in enumerate(range(lo - 3, hi + 3)):
            if x < 0:
                column = low_ref[0, x + 3]
            elif x >= cols:
                column = high_ref[0, x - cols]
            else:
                column = mid_ref[0, x]
            ext[s, k * cin : k * cin + nvars, :] = column
        for x in range(hi - lo + 4):
            v = conv_column(ext.at[s], w1_ref[...], x, cin, hid, first_h, last_h)
            a1[s, x * hid : (x + 1) * hid, :] = silu(v).astype(jnp.bfloat16)
        for x in range(hi - lo + 2):
            v = conv_column(a1.at[s], w2_ref[...], x, hid, hid, first_h, last_h)
            a2[s, x * hid : (x + 1) * hid, :] = silu(v).astype(jnp.bfloat16)
        for x in range(hi - lo):
            noise = conv_column(a2.at[s], w3_ref[...], x, hid, cin, first_o, last_o)[:nvars]
            current = ext[s, (x + 3) * cin : (x + 4) * cin, :].astype(jnp.float32)[:nvars]
            seen = obs_ref[lo + x].astype(jnp.float32)
            gain = 0.25 * ow_ref[lo + x]
            new = current - 0.5 * noise + gain * (seen - current)
            out_ref[0, at] = new.astype(jnp.bfloat16)
            at += 1


def update_chunk(spans, edges, mid, observed, obs_weight, w1, w2, w3, cin, hid):
    slots, _, nvars, lat = mid.shape
    step = sum(hi - lo for lo, hi in spans)
    widest = max(hi - lo for lo, hi in spans)
    whole = lambda a: pl.BlockSpec(a.shape, lambda p: (0,) * a.ndim)
    own = lambda a: pl.BlockSpec((1,) + a.shape[1:], lambda p: (p, 0, 0, 0))
    return pl.pallas_call(
        functools.partial(step_kernel, spans, cin, hid, bool(edges)),
        out_shape=jax.ShapeDtypeStruct((slots, step, nvars, lat), jnp.bfloat16),
        grid=(slots,),
        in_specs=[own(a) for a in (*edges, mid)]
        + [whole(a) for a in (observed, obs_weight, w1, w2, w3)],
        out_specs=pl.BlockSpec((1, step, nvars, lat), lambda p: (p, 0, 0, 0)),
        scratch_shapes=[
            pltpu.VMEM((len(spans), (widest + 6) * cin, lat), jnp.bfloat16),
            pltpu.VMEM((len(spans), (widest + 4) * hid, lat), jnp.bfloat16),
            pltpu.VMEM((len(spans), (widest + 2) * hid, lat), jnp.bfloat16),
        ],
        compiler_params=pltpu.CompilerParams(vmem_limit_bytes=56 << 20),
        cost_estimate=pl.CostEstimate(flops=0, bytes_accessed=1024, transcendentals=0),
        name="update_chunk",
    )(*edges, mid, observed, obs_weight, w1, w2, w3)


def exchange_kernel(n_lon, mid_ref, sums_ref, low_ref, high_ref, total_ref, parts, edge_send, edge_recv, lon_send, lon_recv):
    lon = lax.axis_index("lon")
    cols = mid_ref.shape[1]

    def lon_at(k):
        return {"lon": lax.rem(lon + k, n_lon)}

    barrier = pltpu.get_barrier_semaphore()
    for k in range(1, n_lon):
        pl.semaphore_signal(barrier, inc=1, device_id=lon_at(k), device_id_type=pl.DeviceIdType.MESH)
    pl.semaphore_wait(barrier, n_lon - 1)

    def send(src, dst, s, r, target):
        copy = pltpu.make_async_remote_copy(
            src_ref=src, dst_ref=dst, send_sem=s, recv_sem=r,
            device_id=target, device_id_type=pl.DeviceIdType.MESH,
        )
        copy.start()
        return copy

    edges = [
        send(mid_ref.at[:, cols - 3 : cols], low_ref, edge_send.at[0], edge_recv.at[0], lon_at(1)),
        send(mid_ref.at[:, 0:3], high_ref, edge_send.at[1], edge_recv.at[1], lon_at(n_lon - 1)),
    ]
    parts[lon] = sums_ref[...]
    over_lon = [
        send(sums_ref, parts.at[lon], lon_send.at[k - 1], lon_recv.at[k - 1], lon_at(k))
        for k in range(1, n_lon)
    ]
    for copy in over_lon:
        copy.wait()
    band_sum = parts[0]
    for k in range(1, n_lon):
        band_sum = band_sum + parts[k]
    total_ref[...] = band_sum
    for copy in edges:
        copy.wait()


def exchange(mid, sums, n_lon):
    slots, _, nvars, lat = mid.shape
    edge = jax.ShapeDtypeStruct((slots, 3, nvars, lat), mid.dtype)
    vmem = pl.BlockSpec(memory_space=pltpu.VMEM)
    return pl.pallas_call(
        functools.partial(exchange_kernel, n_lon),
        out_shape=(edge, edge, jax.ShapeDtypeStruct(sums.shape, jnp.float32)),
        in_specs=[pl.BlockSpec(memory_space=pl.ANY), vmem],
        out_specs=(vmem, vmem, vmem),
        scratch_shapes=[
            pltpu.VMEM((n_lon,) + sums.shape, jnp.float32),
            pltpu.SemaphoreType.DMA((2,)),
            pltpu.SemaphoreType.DMA((2,)),
            pltpu.SemaphoreType.DMA((n_lon - 1,)),
            pltpu.SemaphoreType.DMA((n_lon - 1,)),
        ],
        compiler_params=pltpu.CompilerParams(collective_id=0, has_side_effects=True),
        cost_estimate=pl.CostEstimate(flops=0, bytes_accessed=1024, transcendentals=0),
        name="exchange",
    )(mid, sums)


def across(u):
    n = lax.axis_size("dom")
    return [u] + [
        lax.ppermute(u, "dom", [(d, (d + 2 * k) % n) for d in range(n)]) for k in range(1, n // 2)
    ]


def pick_kernel(slots, base, codes_ref, *refs):
    *pieces, out_ref = refs
    if base == 0:
        received_ref, *pieces = pieces
    for s in range(slots):
        for m in range(len(pieces) * slots):
            wanted = codes_ref[base + s] == m
            if base == 0:
                wanted = wanted & (codes_ref[2 * slots + s] == 1)

            @pl.when(wanted)
            def _():
                out_ref[s] = pieces[m // slots][m % slots]

        if base == 0:

            @pl.when(codes_ref[2 * slots + s] == 0)
            def _():
                out_ref[s] = received_ref[s]


def pick(codes, base, arrays):
    u = arrays[0]
    slots = u.shape[0]
    vmem = pl.BlockSpec(memory_space=pltpu.VMEM)
    return pl.pallas_call(
        functools.partial(pick_kernel, slots, base),
        out_shape=jax.ShapeDtypeStruct(u.shape, u.dtype),
        in_specs=[pl.BlockSpec(memory_space=pltpu.SMEM)] + [vmem] * len(arrays),
        out_specs=vmem,
        compiler_params=pltpu.CompilerParams(vmem_limit_bytes=24 << 20),
        cost_estimate=pl.CostEstimate(flops=0, bytes_accessed=1024, transcendentals=0),
        name="pick",
    )(codes, *arrays)


def weight_kernel(slots, t_ref, *refs):
    *part_refs, out_ref = refs
    shape = out_ref.shape
    real = lax.broadcasted_iota(jnp.int32, shape, 0) < slots
    count = len(part_refs) * slots

    def over_particles(rows):
        total = rows[0]
        for row in rows[1:]:
            total = total + row
        return jnp.sum(total, axis=0, keepdims=True)

    misfits = [jnp.broadcast_to(jnp.sum(r[...], axis=1, keepdims=True), shape) for r in part_refs]
    center = over_particles([jnp.where(real, m, 0.0) for m in misfits]) / count
    deviations = [jnp.where(real, m - center, 0.0) for m in misfits]
    spread = jnp.sqrt(over_particles([d * d for d in deviations]) / count + 1.0)
    expos = [jnp.where(real, jnp.exp(-0.5 * t_ref[0] * d / spread), 0.0) for d in deviations]
    out_ref[...] = expos[0] / over_particles(expos)


def own_weights_of(parts, tempering, slots):
    vmem = pl.BlockSpec(memory_space=pltpu.VMEM)
    out = pl.pallas_call(
        functools.partial(weight_kernel, slots),
        out_shape=jax.ShapeDtypeStruct(parts[0].shape, jnp.float32),
        in_specs=[pl.BlockSpec(memory_space=pltpu.SMEM)] + [vmem] * len(parts),
        out_specs=vmem,
        name="own_weights",
    )(tempering, *parts)
    return out[:slots, 0]


def many_chips(particles, observed, precision, stations, ancestors, tempering, w_in, w_mid, w_out):
    slots, nvars, cols, lat = particles.shape
    hid = w_mid.shape[2]
    cin = pad_to(nvars, 16)
    n_dom, n_lon = lax.axis_size("dom"), lax.axis_size("lon")
    me = lax.axis_index("dom")
    mid = particles.transpose(0, 2, 1, 3)
    sibling_anc = lax.ppermute(ancestors, "dom", [(d, d ^ 1) for d in range(n_dom)])

    obs_weight = stations.astype(jnp.float32) * precision
    wanted = jnp.concatenate([ancestors, sibling_anc])
    owner = lax.div(wanted, slots)
    chips = n_dom // 2
    steps = lax.rem(lax.shift_right_logical(me, 1) - lax.div(owner, 2) + chips, chips)
    candidate = steps * slots + lax.rem(wanted, slots)
    here = lax.rem(owner, 2) == (me & 1)

    obs_columns = observed.transpose(1, 0, 2)
    ow_columns = obs_weight[:, None, :]
    w1 = stacked_taps(w_in, hid, cin)
    w2 = stacked_taps(w_mid, hid, hid)
    w3 = stacked_taps(w_out, cin, hid)

    update = lambda spans, edges: update_chunk(
        spans, edges, mid, obs_columns, ow_columns, w1, w2, w3, cin, hid
    )
    u = update([(3, cols - 3)], [])
    groups = [across(u)]

    late_weight, _ = lax.optimization_barrier((obs_weight, u))
    misfit_cell = particles.astype(jnp.float32) - observed.astype(jnp.float32)[None]
    local_sums = jnp.sum(late_weight[None, None] * misfit_cell * misfit_cell, axis=(1, 2))
    sums = jnp.sum(local_sums.reshape(slots, lat // 128, 128), axis=1)
    sums = jnp.pad(sums, ((0, pad_to(slots, 8) - slots), (0, 0)))
    low, high, band_sums = exchange(mid, sums, n_lon)
    groups.append(across(update([(0, 3), (cols - 3, cols)], [low, high])))

    parts = [band_sums] + [
        lax.ppermute(band_sums, "dom", [(d, (d + k) % n_dom) for d in range(n_dom)])
        for k in range(1, n_dom)
    ]
    own_weights = own_weights_of(parts, tempering, slots)

    codes = jnp.concatenate([candidate, here[:slots].astype(jnp.int32)])
    groups = lax.optimization_barrier(groups)
    results = []
    for pieces in groups:
        sent = pick(codes, slots, pieces)
        received = lax.ppermute(sent, "dom", [(d, d ^ 1) for d in range(n_dom)])
        results.append(pick(codes, 0, [received, *pieces]))
    inner, sides = results
    new_columns = jnp.concatenate([sides[:, :3], inner, sides[:, 3:]], axis=1)
    return (new_columns.transpose(0, 2, 1, 3), own_weights)


MESH = pl.DeviceIdType.MESH
FIXED = 2


def column_chunks(cols):
    middle = cols // 2
    chunks = [[middle - 1, middle]]
    above, below = list(range(middle + 1, cols - 3)), list(range(3, middle - 1))
    for side, take in ((above, lambda v, k: v[:k]), (below, lambda v, k: v[-k:])):
        left = side
        while left:
            size = 4 if len(left) >= 6 or len(left) == 4 else min(len(left), 6)
            part = take(left, size)
            chunks.append(part)
            left = [x for x in left if x not in part]
    return chunks


def remote(src, dst, s, r, target):
    copy = pltpu.make_async_remote_copy(
        src_ref=src, dst_ref=dst, send_sem=s, recv_sem=r, device_id=target, device_id_type=MESH
    )
    copy.start()
    return copy


def main_kernel(n_lon, n_ens, cin, hid, chunks, *refs):
    (part_hbm, obs_hbm, prec_hbm, stat_hbm, anc_hbm, temp_hbm, win_hbm, wmid_hbm, wout_hbm,
     out_ref, spare_ref, info_ref, wts_ref,
     raw, raw_obs, prec_ref, stat_ref, anc_ref, temp_ref, win_ref, wmid_ref, wout_ref, ext, obs_cm, a1, a2, w1, w2, w3, gain, misfit, anc_own, anc_all, k_own, k_all,
     lon_sum, lon_parts, dom_parts, halo_out, halo_in, *rest) = refs
    inner = len(chunks)
    n = inner + 2
    mine, gathered, arrived = rest[:n], rest[n : 2 * n], rest[2 * n : 3 * n]
    (load_sem, anc_s, anc_r, halo_s, halo_r, sib_s, sib_r, x_s, x_r, fwd_s, fwd_r,
     lon_s, lon_r, dom_s, dom_r, ens_s, ens_r, from_low, from_high) = rest[3 * n :]
    slots, nvars, cols, lat = part_hbm.shape
    rows = spare_ref.shape[2]
    f32, bf16 = jnp.float32, jnp.bfloat16

    dom, lon, ens = lax.axis_index("dom"), lax.axis_index("lon"), lax.axis_index("ens")
    core, chip = lax.rem(dom, 2), lax.div(dom, 2)
    sibling, partner = {"dom": dom + 1 - 2 * core}, {"dom": lax.rem(dom + 2, 4)}

    def lon_at(k):
        return {"lon": lax.rem(lon + k, n_lon)}

    def dom_at(k):
        return {"dom": lax.rem(dom + k, 4)}

    def ens_at(k):
        return {"ens": lax.rem(ens + k, n_ens)}

    peers = [dom_at(k) for k in range(1, 4)] + [ens_at(k) for k in range(1, n_ens)]
    barrier = pltpu.get_barrier_semaphore()
    for peer in peers:
        pl.semaphore_signal(barrier, inc=1, device_id=peer, device_id_type=MESH)

    @pl.when(lon < n_lon - 1)
    def _():
        pl.semaphore_signal(barrier, inc=1, device_id=lon_at(1), device_id_type=MESH)

    @pl.when(lon > 0)
    def _():
        pl.semaphore_signal(barrier, inc=1, device_id=lon_at(n_lon - 1), device_id_type=MESH)

    def load(src, dst, i):
        copy = pltpu.make_async_copy(src, dst, load_sem.at[i])
        copy.start()
        return copy

    names = [
        (anc_hbm, anc_ref), (win_hbm, win_ref), (wmid_hbm, wmid_ref), (wout_hbm, wout_ref),
        (prec_hbm, prec_ref), (stat_hbm, stat_ref), (temp_hbm, temp_ref),
    ]
    small = [load(src, dst, slots + 1 + i) for i, (src, dst) in enumerate(names)]
    states = [load(part_hbm.at[p], raw.at[p], p) for p in range(slots)]
    seen = load(obs_hbm, raw_obs, slots)

    w1[...] = jnp.zeros_like(w1)
    w3[...] = jnp.zeros_like(w3)
    misfit[...] = jnp.zeros_like(misfit)
    small[0].wait()
    for s in range(slots):
        anc_own[s] = anc_ref[s]
        anc_all[dom, s] = anc_ref[s]

    @pl.when((lon > 0) & (lon < n_lon - 1))
    def _():
        pl.semaphore_wait(barrier, len(peers) + 2)

    @pl.when((lon == 0) | (lon == n_lon - 1))
    def _():
        pl.semaphore_wait(barrier, len(peers) + 1)

    sent_anc = [
        remote(anc_own, anc_all.at[dom], anc_s.at[k - 1], anc_r.at[k - 1], dom_at(k))
        for k in range(1, 4)
    ]
    @pl.when(lon == 0)
    def _():
        pl.semaphore_signal(from_low, inc=1, device_id=lon_at(1), device_id_type=MESH)

    @pl.when(lon == n_lon - 1)
    def _():
        pl.semaphore_signal(from_high, inc=1, device_id=lon_at(n_lon - 1), device_id_type=MESH)

    def relay(r):
        @pl.when(lon == r)
        def _():
            pl.semaphore_wait(from_low, 1)
            if r < n_lon - 1:
                pl.semaphore_signal(from_low, inc=1, device_id=lon_at(1), device_id_type=MESH)

        @pl.when(lon == n_lon - 1 - r)
        def _():
            pl.semaphore_wait(from_high, 1)
            if r < n_lon - 1:
                pl.semaphore_signal(from_high, inc=1, device_id=lon_at(n_lon - 1), device_id_type=MESH)

    def turn(src, dst, at, x0):
        width = 8
        for q in range(0, cin, 16):
            count = min(16, nvars - q)
            v = src[q : q + count, x0 : x0 + width, :].astype(f32)
            if count < 16:
                v = jnp.concatenate([v, jnp.zeros((16 - count, width, lat), f32)], axis=0)
            dst[at + x0 : at + x0 + width, q : q + 16, :] = jnp.swapaxes(v, 0, 1).astype(bf16)

    middle = 8 * (cols // 16)
    outer = [x0 for x0 in range(0, cols, 8) if x0 != middle]
    for p in range(slots):
        states[p].wait()
        for x0 in outer:
            turn(raw.at[p], ext.at[p], 3, x0)
    for p in range(slots):
        for t in range(3):
            halo_out[0, p, t] = ext[p, cols + t, :rows]
            halo_out[1, p, t] = ext[p, 3 + t, :rows]
            if rows < cin:
                ext[p, t] = jnp.zeros((cin, lat), bf16)
                ext[p, cols + 3 + t] = jnp.zeros((cin, lat), bf16)

    def edge(up, start):
        if up:
            src, dst, k, target = halo_out.at[0], halo_in.at[0], 0, lon_at(1)
        else:
            src, dst, k, target = halo_out.at[1], halo_in.at[1], 1, lon_at(n_lon - 1)
        copy = pltpu.make_async_remote_copy(
            src_ref=src, dst_ref=dst, send_sem=halo_s.at[k], recv_sem=halo_r.at[k],
            device_id=target, device_id_type=MESH,
        )
        if start:
            copy.start()
        return copy

    @pl.when(lon < n_lon - 1)
    def _():
        edge(True, True)

    @pl.when(lon > 0)
    def _():
        edge(False, True)

    relay(1)
    for copy in small[1:]:
        copy.wait()
    for j in range(3):
        for i in range(3):
            w1[j * hid : (j + 1) * hid, i * cin : i * cin + nvars] = win_ref[i, j]
            w2[j * hid : (j + 1) * hid, i * hid : (i + 1) * hid] = wmid_ref[i, j]
            turned = wout_ref[i, j].astype(f32).T
            w3[j * cin : j * cin + nvars, i * hid : (i + 1) * hid] = turned.astype(bf16)
    gain[...] = 0.25 * (stat_ref[...].astype(f32) * prec_ref[...])

    relay(2)
    for p in range(slots):
        turn(raw.at[p], ext.at[p], 3, middle)
    seen.wait()
    turn(raw_obs, obs_cm, 0, middle)

    lane_h = lax.broadcasted_iota(jnp.int32, (hid, lat), 1)
    lane_o = lax.broadcasted_iota(jnp.int32, (cin, lat), 1)
    edges_h = (lane_h == 0, lane_h == lat - 1)
    edges_o = (lane_o == 0, lane_o == lat - 1)

    def conv(src, w, x, out_rows, edges):
        window = src[pl.ds(x, 3)]
        window = window.reshape(window.shape[0] * window.shape[1], lat)
        v = jnp.dot(w[...], window, preferred_element_type=f32)
        below = pltpu.roll(v[:out_rows], 1, 1)
        above = pltpu.roll(v[2 * out_rows :], lat - 1, 1)
        return (
            v[out_rows : 2 * out_rows]
            + jnp.where(edges[0], 0.0, below)
            + jnp.where(edges[1], 0.0, above)
        )

    def first(p, x):
        a1[p, x + 2] = silu(conv(ext.at[p], w1, x + 2, hid, edges_h)).astype(bf16)

    def second(p, x):
        a2[p, x + 1] = silu(conv(a1.at[p], w2, x + 1, hid, edges_h)).astype(bf16)

    def third(p, x, dst, at):
        noise = conv(a2.at[p], w3, x, cin, edges_o)
        current = ext[p, x + 3].astype(f32)
        diff = obs_cm[x].astype(f32) - current
        pull = gain[pl.ds(x, 1), :] * diff
        new = current - 0.5 * noise + pull
        dst[p, at] = new[:rows].astype(bf16)
        square = pull * diff
        total = square[0:8]
        for r in range(8, cin, 8):
            total = total + square[r : r + 8]
        misfit[p] += total

    def share(c):
        return remote(mine[c].at[0:slots], mine[c].at[slots : 2 * slots], sib_s.at[c], sib_r.at[c], sibling)

    def choose():
        theirs = [anc_all[2 * (1 - chip) + i, s] for i in range(2) for s in range(slots)]
        ours = [anc_all[2 * chip + i, s] for i in range(2) for s in range(slots)]
        group = 2 * slots
        one, zero = jnp.int32(1), jnp.int32(0)

        def wanted(ids, base):
            flags = []
            for r in range(group):
                flag = zero
                for g in ids:
                    flag = jnp.where(g == base + r, one, flag)
                flags.append(flag)
            return flags

        give = wanted(theirs, group * chip)
        take = wanted(ours, group * (1 - chip))
        order, count = [zero] * group, zero
        for r in range(group):
            for j in range(r + 1):
                order[j] = jnp.where((count == j) & (give[r] == 1), jnp.int32(r), order[j])
            count = count + give[r]
        near = [jnp.where(lax.div(r, slots) == core, zero, jnp.int32(slots)) + lax.rem(r, slots) for r in order]
        ranks, got = [], zero
        for r in range(group):
            ranks.append(got)
            got = got + take[r]
        sources, remotes = [], []
        for s in range(slots):
            g = anc_ref[s]
            r = g - group * lax.div(g, group)
            rank = zero
            for m in range(group):
                rank = jnp.where(r == m, ranks[m], rank)
            local = jnp.where(lax.div(r, slots) == core, zero, jnp.int32(slots)) + lax.rem(r, slots)
            sources.append(jnp.where(lax.div(g, group) == chip, local, group + rank))
            remotes.append(r)
        return near, sources, remotes, jnp.maximum(count, got)

    state = {}

    def pass_on(c, shared):
        shared.wait()
        if c >= inner:
            chosen = jnp.where(core == 0, state["near"][0], state["near"][1])
            for t in range(3):
                gathered[c][t] = mine[c][chosen, t]
            base = sum(len(chunk) for chunk in chunks[1:]) // 2
            if c == n - 1:
                for j in range(FIXED, 2 * slots):
                    for t in range(3):
                        spare_ref[j - FIXED, base + t] = jnp.where(
                            core == 0, mine[inner][state["near"][j], t], mine[c][state["near"][j], t]
                        )
            return remote(gathered[c], arrived[c].at[core], x_s.at[c], x_r.at[c], partner)
        half = len(chunks[c]) // 2
        start = core * half
        for j in range(FIXED):
            for t in range(half):
                gathered[c][j, t] = mine[c][state["near"][j], start + t]
        base = sum(len(chunk) for chunk in chunks[1:c]) // 2
        for j in range(FIXED, 2 * slots):
            for t in range(half):
                spare_ref[j - FIXED, base + t] = mine[c][state["near"][j], start + t]
        return remote(gathered[c], arrived[c].at[core], x_s.at[c], x_r.at[c], partner)

    ready = [set(), set()]

    def compute(c):
        one = sorted({x + d for x in chunks[c] for d in range(-2, 3)} - ready[0])
        two = sorted({x + d for x in chunks[c] for d in range(-1, 2)} - ready[1])
        ready[0].update(one)
        ready[1].update(two)
        for x in one:
            for p in range(slots):
                first(p, x)
        for x in two:
            for p in range(slots):
                second(p, x)
        for at, x in enumerate(chunks[c]):
            for p in range(slots):
                third(p, x, mine[c], at)

    first_side = jnp.where(lon == 0, 1, 0)
    sides = {inner: first_side, inner + 1: 1 - first_side}

    def compute_edge(c):
        side = sides[c]
        for t in range(3):
            for p in range(slots):
                first(p, side * (cols + 1) - 2 + t)
        for t in range(3):
            for p in range(slots):
                second(p, side * (cols - 1) - 1 + t)
        for t in range(3):
            for p in range(slots):
                third(p, side * (cols - 3) + t, mine[c], t)

    compute(0)
    ends = pl.ds(core * slots, slots)
    crossings = [
        remote(mine[0].at[0:slots], arrived[0].at[ends], x_s.at[0], x_r.at[0], partner)
    ]

    shares = [share(0)]
    for r in range(3, n_lon):
        relay(r)

    @pl.when(lon == n_lon - 1)
    def _():
        edge(True, True)

    @pl.when(lon == 0)
    def _():
        edge(False, True)

    for x0 in outer:
        turn(raw_obs, obs_cm, 0, x0)
    compute(1)
    shares.append(share(1))
    for copy in sent_anc:
        copy.wait()
    near, sources, remotes, most = choose()
    k_own[0] = most
    state["near"], state["sources"], state["remotes"] = near, sources, remotes
    state["ens"] = [
        remote(k_own, k_all.at[k - 1], ens_s.at[k - 1], ens_r.at[k - 1], ens_at(k))
        for k in range(1, n_ens)
    ]
    shares[0].wait()
    crossings.append(pass_on(1, shares[1]))
    compute(2)
    shares.append(share(2))
    crossings.append(pass_on(2, shares[2]))
    for c in range(3, inner):
        compute(c)
        shares.append(share(c))
        if c > 3:
            crossings.append(pass_on(c - 1, shares[c - 1]))
    for c in (inner, inner + 1):
        @pl.when(sides[c] == 0)
        def _():
            edge(True, False).wait_recv()
            for p in range(slots):
                for t in range(3):
                    ext[p, t, :rows] = halo_in[0, p, t]

        @pl.when(sides[c] == 1)
        def _():
            edge(False, False).wait_recv()
            for p in range(slots):
                for t in range(3):
                    ext[p, cols + 3 + t, :rows] = halo_in[1, p, t]

        compute_edge(c)
        shares.append(share(c))
        if c == inner:
            crossings.append(pass_on(c - 1, shares[c - 1]))
        crossings.append(pass_on(c, shares[c]))
    edge(True, False).wait_send()
    edge(False, False).wait_send()

    sums = [jnp.sum(misfit[p], axis=0, keepdims=True) for p in range(slots)]
    sums = [s[:, :128] + s[:, 128:] for s in sums]
    row = lax.broadcasted_iota(jnp.int32, (8, 128), 0)
    local = jnp.zeros((8, 128), f32)
    for p in range(slots):
        local = jnp.where(row == p, sums[p], local)
    lon_sum[...] = 4.0 * local
    sent = [
        remote(lon_sum, lon_parts.at[k - 1], lon_s.at[k - 1], lon_r.at[k - 1], lon_at(k))
        for k in range(1, n_lon)
    ]
    forwards = []

    def finish(c):
        forwards[c].wait()
        half = len(chunks[c]) // 2 if c < inner else 0
        for s in range(slots):
            src = state["sources"][s]
            near = jnp.minimum(src, 2 * slots - 1)
            far = jnp.clip(src - 2 * slots, 0, FIXED - 1)
            if c >= inner:
                for at in range(3):
                    out_ref[s, sides[c] * (cols - 3) + at] = jnp.where(
                        src < 2 * slots, mine[c][near, at], arrived[c][far, at]
                    )[:nvars]
                continue
            for at, x in enumerate(chunks[c]):
                if c == 0:
                    far_away = arrived[c][state["remotes"][s], at]
                else:
                    far_away = arrived[c][at // half, far, at % half]
                out_ref[s, x] = jnp.where(src < 2 * slots, mine[c][near, at], far_away)[:nvars]

    for c in range(n):
        crossings[c].wait()
        piece = arrived[c].at[ends if c == 0 else core]
        forwards.append(remote(piece, piece, fwd_s.at[c], fwd_r.at[c], sibling))
        if c == n - 3:
            for copy in sent:
                copy.wait()
            band = lon_sum[...]
            for k in range(1, n_lon):
                band = band + lon_parts[k - 1]
            dom_parts[0] = band
            sent = [
                remote(dom_parts.at[0], dom_parts.at[k], dom_s.at[k - 1], dom_r.at[k - 1], dom_at(k))
                for k in range(1, 4)
            ]
        if c > 0:
            finish(c - 1)
    for copy in sent:
        copy.wait()
    misfits = [jnp.broadcast_to(jnp.sum(dom_parts[k], axis=1, keepdims=True), (8, 128)) for k in range(4)]
    real = row < slots

    def over(values):
        total = values[0]
        for value in values[1:]:
            total = total + value
        return jnp.sum(jnp.where(real, total, 0.0), axis=0, keepdims=True)

    center = over(misfits) / (4 * slots)
    off = [m - center for m in misfits]
    spread = jnp.sqrt(over([d * d for d in off]) / (4 * slots) + 1.0)
    expos = [jnp.exp(-0.5 * temp_ref[0] * d / spread) for d in off]
    own = expos[0] / over(expos)
    lane = lax.broadcasted_iota(jnp.int32, (8, 128), 1)
    for s in range(slots):
        wts_ref[s] = jnp.sum(jnp.where((row == s) & (lane == 0), own, 0.0))
    finish(n - 1)

    most = k_own[0]
    for copy in state["ens"]:
        copy.wait()
    for k in range(1, n_ens):
        most = jnp.maximum(most, k_all[k - 1, 0])
    info_ref[0] = jnp.maximum(most - FIXED, 0)
    for s in range(slots):
        info_ref[1 + s] = state["sources"][s]


def main_call(particles, observed, precision, stations, ancestors, tempering, w_in, w_mid, w_out):
    slots, nvars, cols, lat = particles.shape
    hid = w_mid.shape[2]
    cin, rows = pad_to(nvars, 16), pad_to(nvars, 8)
    n_lon, n_ens = lax.axis_size("lon"), lax.axis_size("ens")
    chunks = column_chunks(cols)
    n = len(chunks) + 2
    bf16, f32 = jnp.bfloat16, jnp.float32
    vmem = pl.BlockSpec(memory_space=pltpu.VMEM)
    smem = pl.BlockSpec(memory_space=pltpu.SMEM)
    hbm = pl.BlockSpec(memory_space=pltpu.HBM)
    dma = pltpu.SemaphoreType.DMA
    scratch = [
        pltpu.VMEM((slots, nvars, cols, lat), bf16),
        pltpu.VMEM((nvars, cols, lat), bf16),
        pltpu.VMEM(precision.shape, f32),
        pltpu.VMEM(stations.shape, jnp.int32),
        pltpu.SMEM(ancestors.shape, jnp.int32),
        pltpu.SMEM(tempering.shape, f32),
        pltpu.VMEM(w_in.shape, bf16),
        pltpu.VMEM(w_mid.shape, bf16),
        pltpu.VMEM((3, 3) + w_out.shape[:1:-1], bf16),
        pltpu.VMEM((slots, cols + 6, cin, lat), bf16),
        pltpu.VMEM((cols, cin, lat), bf16),
        pltpu.VMEM((slots, cols + 4, hid, lat), bf16),
        pltpu.VMEM((slots, cols + 2, hid, lat), bf16),
        pltpu.VMEM((3 * hid, 3 * cin), bf16),
        pltpu.VMEM((3 * hid, 3 * hid), bf16),
        pltpu.VMEM((3 * cin, 3 * hid), bf16),
        pltpu.VMEM((cols, lat), f32),
        pltpu.VMEM((slots, 8, lat), f32),
        pltpu.SMEM((128,), jnp.int32),
        pltpu.SMEM((4, 128), jnp.int32),
        pltpu.SMEM((128,), jnp.int32),
        pltpu.SMEM((max(n_ens - 1, 1), 128), jnp.int32),
        pltpu.VMEM((8, 128), f32),
        pltpu.VMEM((max(n_lon - 1, 1), 8, 128), f32),
        pltpu.VMEM((4, 8, 128), f32),
        pltpu.VMEM((2, slots, 3, rows, lat), bf16),
        pltpu.VMEM((2, slots, 3, rows, lat), bf16),
    ]
    scratch += [pltpu.VMEM((2 * slots, len(c), rows, lat), bf16) for c in chunks]
    scratch += [pltpu.VMEM((2 * slots, 3, rows, lat), bf16)] * 2
    scratch += [pltpu.VMEM((FIXED, len(c) // 2, rows, lat), bf16) for c in chunks]
    scratch += [pltpu.VMEM((3, rows, lat), bf16)] * 2
    scratch += [pltpu.VMEM((2 * slots, len(chunks[0]), rows, lat), bf16)]
    scratch += [pltpu.VMEM((2, FIXED, len(c) // 2, rows, lat), bf16) for c in chunks[1:]]
    scratch += [pltpu.VMEM((2, 3, rows, lat), bf16)] * 2
    scratch += [dma((slots + 8,))] + [dma((3,))] * 2 + [dma((2,))] * 2 + [dma((n,))] * 6
    scratch += [dma((max(n_lon - 1, 1),))] * 2 + [dma((3,))] * 2 + [dma((max(n_ens - 1, 1),))] * 2
    scratch += [pltpu.SemaphoreType.REGULAR] * 2
    return pl.pallas_call(
        functools.partial(main_kernel, n_lon, n_ens, cin, hid, chunks),
        out_shape=(
            jax.ShapeDtypeStruct((slots, cols, nvars, lat), bf16),
            jax.ShapeDtypeStruct((2 * slots - FIXED, (cols - len(chunks[0])) // 2, rows, lat), bf16),
            jax.ShapeDtypeStruct((1 + slots,), jnp.int32),
            jax.ShapeDtypeStruct((slots,), f32),
        ),
        in_specs=[hbm] * 9,
        out_specs=(vmem, vmem, smem, smem),
        scratch_shapes=scratch,
        compiler_params=pltpu.CompilerParams(
            collective_id=0, has_side_effects=True, vmem_limit_bytes=62 << 20
        ),
        name="step",
    )(particles, observed, precision, stations, ancestors, tempering, w_in, w_mid, w_out.transpose(0, 1, 3, 2))


def more_kernel(extra, chunks, info_ref, out_in, spare_ref, out_ref, *rest):
    arrived, (x_s, x_r, fwd_s, fwd_r) = rest[: len(chunks)], rest[len(chunks) :]
    slots = out_in.shape[0]
    nvars = out_in.shape[2]
    dom = lax.axis_index("dom")
    core = lax.rem(dom, 2)
    sibling, partner = {"dom": dom + 1 - 2 * core}, {"dom": lax.rem(dom + 2, 4)}
    barrier = pltpu.get_barrier_semaphore()
    for peer in (sibling, partner):
        pl.semaphore_signal(barrier, inc=1, device_id=peer, device_id_type=MESH)
    pl.semaphore_wait(barrier, 2)
    cols = out_in.shape[1]
    first_side = jnp.where(lax.axis_index("lon") == 0, 1, 0)
    spans, at = [], 0
    for chunk in chunks[1:]:
        spans.append((at, len(chunk) // 2))
        at += len(chunk) // 2
    spans.append((at, 3))
    crossings = []
    for c, (lo, size) in enumerate(spans):
        crossings.append(remote(
            spare_ref.at[0:extra, pl.ds(lo, size)], arrived[c].at[core], x_s.at[c], x_r.at[c], partner
        ))
    sources = [info_ref[1 + s] for s in range(slots)]

    def settle(c):
        lo, size = spans[c]
        for s in range(slots):
            src = sources[s]
            far = jnp.clip(src - (2 * slots + FIXED), 0, extra - 1)
            for half in range(2):
                for t in range(size):
                    if c < len(chunks) - 1:
                        x = chunks[c + 1][half * size + t]
                    else:
                        side = first_side if half == 0 else 1 - first_side
                        x = side * (cols - 3) + t
                    out_ref[s, x] = jnp.where(
                        src < 2 * slots + FIXED, out_in[s, x], arrived[c][half, far, t][:nvars]
                    )

    for s in range(slots):
        for x in chunks[0]:
            out_ref[s, x] = out_in[s, x]
    forwards = []
    for c in range(len(spans)):
        crossings[c].wait()
        piece = arrived[c].at[core]
        forwards.append(remote(piece, piece, fwd_s.at[c], fwd_r.at[c], sibling))
        if c > 0:
            forwards[c - 1].wait()
            settle(c - 1)
    forwards[-1].wait()
    settle(len(spans) - 1)


def more_call(extra, info, out, spare):
    slots, cols, nvars, lat = out.shape
    chunks = column_chunks(cols)
    vmem = pl.BlockSpec(memory_space=pltpu.VMEM)
    dma = pltpu.SemaphoreType.DMA
    return pl.pallas_call(
        functools.partial(more_kernel, extra, chunks),
        out_shape=jax.ShapeDtypeStruct(out.shape, out.dtype),
        in_specs=[pl.BlockSpec(memory_space=pltpu.SMEM), vmem, pl.BlockSpec(memory_space=pltpu.HBM)],
        out_specs=vmem,
        scratch_shapes=[
            pltpu.VMEM((2, extra, size) + spare.shape[2:], out.dtype)
            for size in [len(chunk) // 2 for chunk in chunks[1:]] + [3]
        ] + [dma((len(chunks),))] * 4,
        compiler_params=pltpu.CompilerParams(
            collective_id=extra, has_side_effects=True, vmem_limit_bytes=24 << 20
        ),
        name="more",
    )(info, out, spare)


def two_chips(*args):
    out, spare, info, weights = main_call(*args)
    slots = out.shape[0]
    branches = [lambda info, out, spare: out]
    for extra in range(1, 2 * slots - FIXED + 1):
        branches.append(functools.partial(more_call, extra))
    out = lax.switch(info[0], branches, info, out, spare)
    return (out.transpose(0, 2, 1, 3), weights)


def on_device(*args):
    if lax.axis_size("dom") == 4 and args[0].shape[2] >= 16:
        return two_chips(*args)
    return many_chips(*args)


def solution(mesh):
    return jax.shard_map(
        on_device,
        mesh=mesh,
        in_specs=(
            P(("ens", "dom"), None, "lon", None),
            P("ens", "lon", None),
            P(("ens", "lon"), None),
            P(("ens", "lon"), None),
            P(("ens", "dom")),
            P("ens"),
            P(),
            P(),
            P(),
        ),
        out_specs=(P(("ens", "dom"), None, "lon", None), P(("ens", "dom"))),
        check_vma=False,
    )
```

```python
import functools

import jax
import jax.numpy as jnp
from jax import lax
from jax.experimental import pallas as pl
from jax.experimental.pallas import tpu as pltpu
from jax.sharding import PartitionSpec as P


def pad_to(count, step):
    return -(-count // step) * step


def stacked_taps(weight, out_rows, in_rows):
    _, _, outs, ins = weight.shape
    w = jnp.pad(weight, ((0, 0), (0, 0), (0, out_rows - outs), (0, in_rows - ins)))
    return w.transpose(1, 2, 0, 3).reshape(3 * out_rows, 3 * in_rows)


def conv_column(src_ref, w, x, in_rows, out_rows, first, last):
    window = src_ref[x * in_rows : (x + 3) * in_rows, :]
    p = jnp.dot(w, window, preferred_element_type=jnp.float32)
    lat = p.shape[1]
    below = pltpu.roll(p[:out_rows], 1, 1)
    above = pltpu.roll(p[2 * out_rows :], lat - 1, 1)
    return (
        p[out_rows : 2 * out_rows]
        + jnp.where(first, 0.0, below)
        + jnp.where(last, 0.0, above)
    )


def silu(v):
    half = 0.5 * v
    return half + half * jnp.tanh(half)


def step_kernel(spans, cin, hid, edges, *refs):
    if edges:
        low_ref, high_ref, *refs = refs
    mid_ref, obs_ref, ow_ref, w1_ref, w2_ref, w3_ref, out_ref, ext, a1, a2 = refs
    cols, nvars, lat = mid_ref.shape[1:]
    lane_h = lax.broadcasted_iota(jnp.int32, (hid, lat), 1)
    lane_o = lax.broadcasted_iota(jnp.int32, (cin, lat), 1)
    first_h, last_h = lane_h == 0, lane_h == lat - 1
    first_o, last_o = lane_o == 0, lane_o == lat - 1

    @pl.when(pl.program_id(0) == 0)
    def _():
        ext[...] = jnp.zeros_like(ext)

    at = 0
    for s, (lo, hi) in enumerate(spans):
        for k, x in enumerate(range(lo - 3, hi + 3)):
            if x < 0:
                column = low_ref[0, x + 3]
            elif x >= cols:
                column = high_ref[0, x - cols]
            else:
                column = mid_ref[0, x]
            ext[s, k * cin : k * cin + nvars, :] = column
        for x in range(hi - lo + 4):
            v = conv_column(ext.at[s], w1_ref[...], x, cin, hid, first_h, last_h)
            a1[s, x * hid : (x + 1) * hid, :] = silu(v).astype(jnp.bfloat16)
        for x in range(hi - lo + 2):
            v = conv_column(a1.at[s], w2_ref[...], x, hid, hid, first_h, last_h)
            a2[s, x * hid : (x + 1) * hid, :] = silu(v).astype(jnp.bfloat16)
        for x in range(hi - lo):
            noise = conv_column(a2.at[s], w3_ref[...], x, hid, cin, first_o, last_o)[:nvars]
            current = ext[s, (x + 3) * cin : (x + 4) * cin, :].astype(jnp.float32)[:nvars]
            seen = obs_ref[lo + x].astype(jnp.float32)
            gain = 0.25 * ow_ref[lo + x]
            new = current - 0.5 * noise + gain * (seen - current)
            out_ref[0, at] = new.astype(jnp.bfloat16)
            at += 1


def update_chunk(spans, edges, mid, observed, obs_weight, w1, w2, w3, cin, hid):
    slots, _, nvars, lat = mid.shape
    step = sum(hi - lo for lo, hi in spans)
    widest = max(hi - lo for lo, hi in spans)
    whole = lambda a: pl.BlockSpec(a.shape, lambda p: (0,) * a.ndim)
    own = lambda a: pl.BlockSpec((1,) + a.shape[1:], lambda p: (p, 0, 0, 0))
    return pl.pallas_call(
        functools.partial(step_kernel, spans, cin, hid, bool(edges)),
        out_shape=jax.ShapeDtypeStruct((slots, step, nvars, lat), jnp.bfloat16),
        grid=(slots,),
        in_specs=[own(a) for a in (*edges, mid)]
        + [whole(a) for a in (observed, obs_weight, w1, w2, w3)],
        out_specs=pl.BlockSpec((1, step, nvars, lat), lambda p: (p, 0, 0, 0)),
        scratch_shapes=[
            pltpu.VMEM((len(spans), (widest + 6) * cin, lat), jnp.bfloat16),
            pltpu.VMEM((len(spans), (widest + 4) * hid, lat), jnp.bfloat16),
            pltpu.VMEM((len(spans), (widest + 2) * hid, lat), jnp.bfloat16),
        ],
        compiler_params=pltpu.CompilerParams(vmem_limit_bytes=56 << 20),
        cost_estimate=pl.CostEstimate(flops=0, bytes_accessed=1024, transcendentals=0),
        name="update_chunk",
    )(*edges, mid, observed, obs_weight, w1, w2, w3)


def exchange_kernel(n_lon, mid_ref, sums_ref, low_ref, high_ref, total_ref, parts, edge_send, edge_recv, lon_send, lon_recv):
    lon = lax.axis_index("lon")
    cols = mid_ref.shape[1]

    def lon_at(k):
        return {"lon": lax.rem(lon + k, n_lon)}

    barrier = pltpu.get_barrier_semaphore()
    for k in range(1, n_lon):
        pl.semaphore_signal(barrier, inc=1, device_id=lon_at(k), device_id_type=pl.DeviceIdType.MESH)
    pl.semaphore_wait(barrier, n_lon - 1)

    def send(src, dst, s, r, target):
        copy = pltpu.make_async_remote_copy(
            src_ref=src, dst_ref=dst, send_sem=s, recv_sem=r,
            device_id=target, device_id_type=pl.DeviceIdType.MESH,
        )
        copy.start()
        return copy

    edges = [
        send(mid_ref.at[:, cols - 3 : cols], low_ref, edge_send.at[0], edge_recv.at[0], lon_at(1)),
        send(mid_ref.at[:, 0:3], high_ref, edge_send.at[1], edge_recv.at[1], lon_at(n_lon - 1)),
    ]
    parts[lon] = sums_ref[...]
    over_lon = [
        send(sums_ref, parts.at[lon], lon_send.at[k - 1], lon_recv.at[k - 1], lon_at(k))
        for k in range(1, n_lon)
    ]
    for copy in over_lon:
        copy.wait()
    band_sum = parts[0]
    for k in range(1, n_lon):
        band_sum = band_sum + parts[k]
    total_ref[...] = band_sum
    for copy in edges:
        copy.wait()


def exchange(mid, sums, n_lon):
    slots, _, nvars, lat = mid.shape
    edge = jax.ShapeDtypeStruct((slots, 3, nvars, lat), mid.dtype)
    vmem = pl.BlockSpec(memory_space=pltpu.VMEM)
    return pl.pallas_call(
        functools.partial(exchange_kernel, n_lon),
        out_shape=(edge, edge, jax.ShapeDtypeStruct(sums.shape, jnp.float32)),
        in_specs=[pl.BlockSpec(memory_space=pl.ANY), vmem],
        out_specs=(vmem, vmem, vmem),
        scratch_shapes=[
            pltpu.VMEM((n_lon,) + sums.shape, jnp.float32),
            pltpu.SemaphoreType.DMA((2,)),
            pltpu.SemaphoreType.DMA((2,)),
            pltpu.SemaphoreType.DMA((n_lon - 1,)),
            pltpu.SemaphoreType.DMA((n_lon - 1,)),
        ],
        compiler_params=pltpu.CompilerParams(collective_id=0, has_side_effects=True),
        cost_estimate=pl.CostEstimate(flops=0, bytes_accessed=1024, transcendentals=0),
        name="exchange",
    )(mid, sums)


def across(u):
    n = lax.axis_size("dom")
    return [u] + [
        lax.ppermute(u, "dom", [(d, (d + 2 * k) % n) for d in range(n)]) for k in range(1, n // 2)
    ]


def pick_kernel(slots, base, codes_ref, *refs):
    *pieces, out_ref = refs
    if base == 0:
        received_ref, *pieces = pieces
    for s in range(slots):
        for m in range(len(pieces) * slots):
            wanted = codes_ref[base + s] == m
            if base == 0:
                wanted = wanted & (codes_ref[2 * slots + s] == 1)

            @pl.when(wanted)
            def _():
                out_ref[s] = pieces[m // slots][m % slots]

        if base == 0:

            @pl.when(codes_ref[2 * slots + s] == 0)
            def _():
                out_ref[s] = received_ref[s]


def pick(codes, base, arrays):
    u = arrays[0]
    slots = u.shape[0]
    vmem = pl.BlockSpec(memory_space=pltpu.VMEM)
    return pl.pallas_call(
        functools.partial(pick_kernel, slots, base),
        out_shape=jax.ShapeDtypeStruct(u.shape, u.dtype),
        in_specs=[pl.BlockSpec(memory_space=pltpu.SMEM)] + [vmem] * len(arrays),
        out_specs=vmem,
        compiler_params=pltpu.CompilerParams(vmem_limit_bytes=24 << 20),
        cost_estimate=pl.CostEstimate(flops=0, bytes_accessed=1024, transcendentals=0),
        name="pick",
    )(codes, *arrays)


def weight_kernel(slots, t_ref, *refs):
    *part_refs, out_ref = refs
    shape = out_ref.shape
    real = lax.broadcasted_iota(jnp.int32, shape, 0) < slots
    count = len(part_refs) * slots

    def over_particles(rows):
        total = rows[0]
        for row in rows[1:]:
            total = total + row
        return jnp.sum(total, axis=0, keepdims=True)

    misfits = [jnp.broadcast_to(jnp.sum(r[...], axis=1, keepdims=True), shape) for r in part_refs]
    center = over_particles([jnp.where(real, m, 0.0) for m in misfits]) / count
    deviations = [jnp.where(real, m - center, 0.0) for m in misfits]
    spread = jnp.sqrt(over_particles([d * d for d in deviations]) / count + 1.0)
    expos = [jnp.where(real, jnp.exp(-0.5 * t_ref[0] * d / spread), 0.0) for d in deviations]
    out_ref[...] = expos[0] / over_particles(expos)


def own_weights_of(parts, tempering, slots):
    vmem = pl.BlockSpec(memory_space=pltpu.VMEM)
    out = pl.pallas_call(
        functools.partial(weight_kernel, slots),
        out_shape=jax.ShapeDtypeStruct(parts[0].shape, jnp.float32),
        in_specs=[pl.BlockSpec(memory_space=pltpu.SMEM)] + [vmem] * len(parts),
        out_specs=vmem,
        name="own_weights",
    )(tempering, *parts)
    return out[:slots, 0]


def many_chips(particles, observed, precision, stations, ancestors, tempering, w_in, w_mid, w_out):
    slots, nvars, cols, lat = particles.shape
    hid = w_mid.shape[2]
    cin = pad_to(nvars, 16)
    n_dom, n_lon = lax.axis_size("dom"), lax.axis_size("lon")
    me = lax.axis_index("dom")
    mid = particles.transpose(0, 2, 1, 3)
    sibling_anc = lax.ppermute(ancestors, "dom", [(d, d ^ 1) for d in range(n_dom)])

    obs_weight = stations.astype(jnp.float32) * precision
    wanted = jnp.concatenate([ancestors, sibling_anc])
    owner = lax.div(wanted, slots)
    chips = n_dom // 2
    steps = lax.rem(lax.shift_right_logical(me, 1) - lax.div(owner, 2) + chips, chips)
    candidate = steps * slots + lax.rem(wanted, slots)
    here = lax.rem(owner, 2) == (me & 1)

    obs_columns = observed.transpose(1, 0, 2)
    ow_columns = obs_weight[:, None, :]
    w1 = stacked_taps(w_in, hid, cin)
    w2 = stacked_taps(w_mid, hid, hid)
    w3 = stacked_taps(w_out, cin, hid)

    update = lambda spans, edges: update_chunk(
        spans, edges, mid, obs_columns, ow_columns, w1, w2, w3, cin, hid
    )
    u = update([(3, cols - 3)], [])
    groups = [across(u)]

    late_weight, _ = lax.optimization_barrier((obs_weight, u))
    misfit_cell = particles.astype(jnp.float32) - observed.astype(jnp.float32)[None]
    local_sums = jnp.sum(late_weight[None, None] * misfit_cell * misfit_cell, axis=(1, 2))
    sums = jnp.sum(local_sums.reshape(slots, lat // 128, 128), axis=1)
    sums = jnp.pad(sums, ((0, pad_to(slots, 8) - slots), (0, 0)))
    low, high, band_sums = exchange(mid, sums, n_lon)
    groups.append(across(update([(0, 3), (cols - 3, cols)], [low, high])))

    parts = [band_sums] + [
        lax.ppermute(band_sums, "dom", [(d, (d + k) % n_dom) for d in range(n_dom)])
        for k in range(1, n_dom)
    ]
    own_weights = own_weights_of(parts, tempering, slots)

    codes = jnp.concatenate([candidate, here[:slots].astype(jnp.int32)])
    groups = lax.optimization_barrier(groups)
    results = []
    for pieces in groups:
        sent = pick(codes, slots, pieces)
        received = lax.ppermute(sent, "dom", [(d, d ^ 1) for d in range(n_dom)])
        results.append(pick(codes, 0, [received, *pieces]))
    inner, sides = results
    new_columns = jnp.concatenate([sides[:, :3], inner, sides[:, 3:]], axis=1)
    return (new_columns.transpose(0, 2, 1, 3), own_weights)


MESH = pl.DeviceIdType.MESH
FIXED = 2


def column_chunks(cols):
    middle = cols // 2
    chunks = [[middle - 1, middle]]
    above, below = list(range(middle + 1, cols - 3)), list(range(3, middle - 1))
    for side, take in ((above, lambda v, k: v[:k]), (below, lambda v, k: v[-k:])):
        left = side
        while left:
            size = 4 if len(left) >= 6 or len(left) == 4 else min(len(left), 6)
            part = take(left, size)
            chunks.append(part)
            left = [x for x in left if x not in part]
    return chunks


def remote(src, dst, s, r, target):
    copy = pltpu.make_async_remote_copy(
        src_ref=src, dst_ref=dst, send_sem=s, recv_sem=r, device_id=target, device_id_type=MESH
    )
    copy.start()
    return copy


def main_kernel(n_lon, n_ens, cin, hid, chunks, *refs):
    (part_hbm, obs_hbm, prec_hbm, stat_hbm, anc_hbm, temp_hbm, win_hbm, wmid_hbm, wout_hbm,
     out_ref, spare_ref, info_ref, wts_ref,
     raw, raw_obs, prec_ref, stat_ref, anc_ref, temp_ref, win_ref, wmid_ref, wout_ref, ext, obs_cm, a1, a2, w1, w2, w3, gain, misfit, anc_own, anc_all, k_own, k_all,
     lon_sum, lon_parts, dom_parts, halo_out, halo_in, *rest) = refs
    inner = len(chunks)
    n = inner + 2
    mine, gathered, arrived = rest[:n], rest[n : 2 * n], rest[2 * n : 3 * n]
    (load_sem, anc_s, anc_r, halo_s, halo_r, sib_s, sib_r, x_s, x_r, fwd_s, fwd_r,
     lon_s, lon_r, dom_s, dom_r, ens_s, ens_r, from_low, from_high) = rest[3 * n :]
    slots, nvars, cols, lat = part_hbm.shape
    rows = spare_ref.shape[2]
    f32, bf16 = jnp.float32, jnp.bfloat16

    dom, lon, ens = lax.axis_index("dom"), lax.axis_index("lon"), lax.axis_index("ens")
    core, chip = lax.rem(dom, 2), lax.div(dom, 2)
    sibling, partner = {"dom": dom + 1 - 2 * core}, {"dom": lax.rem(dom + 2, 4)}

    def lon_at(k):
        return {"lon": lax.rem(lon + k, n_lon)}

    def dom_at(k):
        return {"dom": lax.rem(dom + k, 4)}

    def ens_at(k):
        return {"ens": lax.rem(ens + k, n_ens)}

    peers = [dom_at(k) for k in range(1, 4)] + [ens_at(k) for k in range(1, n_ens)]
    barrier = pltpu.get_barrier_semaphore()
    for peer in peers:
        pl.semaphore_signal(barrier, inc=1, device_id=peer, device_id_type=MESH)

    @pl.when(lon < n_lon - 1)
    def _():
        pl.semaphore_signal(barrier, inc=1, device_id=lon_at(1), device_id_type=MESH)

    @pl.when(lon > 0)
    def _():
        pl.semaphore_signal(barrier, inc=1, device_id=lon_at(n_lon - 1), device_id_type=MESH)

    def load(src, dst, i):
        copy = pltpu.make_async_copy(src, dst, load_sem.at[i])
        copy.start()
        return copy

    names = [
        (anc_hbm, anc_ref), (win_hbm, win_ref), (wmid_hbm, wmid_ref), (wout_hbm, wout_ref),
        (prec_hbm, prec_ref), (stat_hbm, stat_ref), (temp_hbm, temp_ref),
    ]
    small = [load(src, dst, slots + 1 + i) for i, (src, dst) in enumerate(names)]
    states = [load(part_hbm.at[p], raw.at[p], p) for p in range(slots)]
    seen = load(obs_hbm, raw_obs, slots)

    w1[...] = jnp.zeros_like(w1)
    w3[...] = jnp.zeros_like(w3)
    misfit[...] = jnp.zeros_like(misfit)
    small[0].wait()
    for s in range(slots):
        anc_own[s] = anc_ref[s]
        anc_all[dom, s] = anc_ref[s]

    @pl.when((lon > 0) & (lon < n_lon - 1))
    def _():
        pl.semaphore_wait(barrier, len(peers) + 2)

    @pl.when((lon == 0) | (lon == n_lon - 1))
    def _():
        pl.semaphore_wait(barrier, len(peers) + 1)

    sent_anc = [
        remote(anc_own, anc_all.at[dom], anc_s.at[k - 1], anc_r.at[k - 1], dom_at(k))
        for k in range(1, 4)
    ]
    @pl.when(lon == 0)
    def _():
        pl.semaphore_signal(from_low, inc=1, device_id=lon_at(1), device_id_type=MESH)

    @pl.when(lon == n_lon - 1)
    def _():
        pl.semaphore_signal(from_high, inc=1, device_id=lon_at(n_lon - 1), device_id_type=MESH)

    def relay(r):
        @pl.when(lon == r)
        def _():
            pl.semaphore_wait(from_low, 1)
            if r < n_lon - 1:
                pl.semaphore_signal(from_low, inc=1, device_id=lon_at(1), device_id_type=MESH)

        @pl.when(lon == n_lon - 1 - r)
        def _():
            pl.semaphore_wait(from_high, 1)
            if r < n_lon - 1:
                pl.semaphore_signal(from_high, inc=1, device_id=lon_at(n_lon - 1), device_id_type=MESH)

    def turn(src, dst, at, x0):
        width = 8
        for q in range(0, cin, 16):
            count = min(16, nvars - q)
            v = src[q : q + count, x0 : x0 + width, :].astype(f32)
            if count < 16:
                v = jnp.concatenate([v, jnp.zeros((16 - count, width, lat), f32)], axis=0)
            dst[at + x0 : at + x0 + width, q : q + 16, :] = jnp.swapaxes(v, 0, 1).astype(bf16)

    middle = 8 * (cols // 16)
    outer = [x0 for x0 in range(0, cols, 8) if x0 != middle]
    for p in range(slots):
        states[p].wait()
        for x0 in outer:
            turn(raw.at[p], ext.at[p], 3, x0)
    for p in range(slots):
        for t in range(3):
            halo_out[0, p, t] = ext[p, cols + t, :rows]
            halo_out[1, p, t] = ext[p, 3 + t, :rows]
            if rows < cin:
                ext[p, t] = jnp.zeros((cin, lat), bf16)
                ext[p, cols + 3 + t] = jnp.zeros((cin, lat), bf16)

    def edge(up, start):
        if up:
            src, dst, k, target = halo_out.at[0], halo_in.at[0], 0, lon_at(1)
        else:
            src, dst, k, target = halo_out.at[1], halo_in.at[1], 1, lon_at(n_lon - 1)
        copy = pltpu.make_async_remote_copy(
            src_ref=src, dst_ref=dst, send_sem=halo_s.at[k], recv_sem=halo_r.at[k],
            device_id=target, device_id_type=MESH,
        )
        if start:
            copy.start()
        return copy

    @pl.when(lon < n_lon - 1)
    def _():
        edge(True, True)

    @pl.when(lon > 0)
    def _():
        edge(False, True)

    relay(1)
    for copy in small[1:]:
        copy.wait()
    for j in range(3):
        for i in range(3):
            w1[j * hid : (j + 1) * hid, i * cin : i * cin + nvars] = win_ref[i, j]
            w2[j * hid : (j + 1) * hid, i * hid : (i + 1) * hid] = wmid_ref[i, j]
            turned = wout_ref[i, j].astype(f32).T
            w3[j * cin : j * cin + nvars, i * hid : (i + 1) * hid] = turned.astype(bf16)
    gain[...] = 0.25 * (stat_ref[...].astype(f32) * prec_ref[...])

    for p in range(slots):
        turn(raw.at[p], ext.at[p], 3, middle)
    seen.wait()
    turn(raw_obs, obs_cm, 0, middle)

    lane_h = lax.broadcasted_iota(jnp.int32, (hid, lat), 1)
    lane_o = lax.broadcasted_iota(jnp.int32, (cin, lat), 1)
    edges_h = (lane_h == 0, lane_h == lat - 1)
    edges_o = (lane_o == 0, lane_o == lat - 1)

    def conv(src, w, x, out_rows, edges):
        window = src[pl.ds(x, 3)]
        window = window.reshape(window.shape[0] * window.shape[1], lat)
        v = jnp.dot(w[...], window, preferred_element_type=f32)
        below = pltpu.roll(v[:out_rows], 1, 1)
        above = pltpu.roll(v[2 * out_rows :], lat - 1, 1)
        return (
            v[out_rows : 2 * out_rows]
            + jnp.where(edges[0], 0.0, below)
            + jnp.where(edges[1], 0.0, above)
        )

    def first(p, x):
        a1[p, x + 2] = silu(conv(ext.at[p], w1, x + 2, hid, edges_h)).astype(bf16)

    def second(p, x):
        a2[p, x + 1] = silu(conv(a1.at[p], w2, x + 1, hid, edges_h)).astype(bf16)

    def third(p, x, dst, at):
        noise = conv(a2.at[p], w3, x, cin, edges_o)
        current = ext[p, x + 3].astype(f32)
        diff = obs_cm[x].astype(f32) - current
        pull = gain[pl.ds(x, 1), :] * diff
        new = current - 0.5 * noise + pull
        dst[p, at] = new[:rows].astype(bf16)
        square = pull * diff
        total = square[0:8]
        for r in range(8, cin, 8):
            total = total + square[r : r + 8]
        misfit[p] += total

    def share(c):
        return remote(mine[c].at[0:slots], mine[c].at[slots : 2 * slots], sib_s.at[c], sib_r.at[c], sibling)

    def choose():
        theirs = [anc_all[2 * (1 - chip) + i, s] for i in range(2) for s in range(slots)]
        ours = [anc_all[2 * chip + i, s] for i in range(2) for s in range(slots)]
        group = 2 * slots
        one, zero = jnp.int32(1), jnp.int32(0)

        def wanted(ids, base):
            flags = []
            for r in range(group):
                flag = zero
                for g in ids:
                    flag = jnp.where(g == base + r, one, flag)
                flags.append(flag)
            return flags

        give = wanted(theirs, group * chip)
        take = wanted(ours, group * (1 - chip))
        order, count = [zero] * group, zero
        for r in range(group):
            for j in range(r + 1):
                order[j] = jnp.where((count == j) & (give[r] == 1), jnp.int32(r), order[j])
            count = count + give[r]
        near = [jnp.where(lax.div(r, slots) == core, zero, jnp.int32(slots)) + lax.rem(r, slots) for r in order]
        ranks, got = [], zero
        for r in range(group):
            ranks.append(got)
            got = got + take[r]
        sources, remotes = [], []
        for s in range(slots):
            g = anc_ref[s]
            r = g - group * lax.div(g, group)
            rank = zero
            for m in range(group):
                rank = jnp.where(r == m, ranks[m], rank)
            local = jnp.where(lax.div(r, slots) == core, zero, jnp.int32(slots)) + lax.rem(r, slots)
            sources.append(jnp.where(lax.div(g, group) == chip, local, group + rank))
            remotes.append(r)
        return near, sources, remotes, jnp.maximum(count, got)

    state = {}

    def pass_on(c, shared):
        shared.wait()
        if c >= inner:
            chosen = jnp.where(core == 0, state["near"][0], state["near"][1])
            for t in range(3):
                gathered[c][t] = mine[c][chosen, t]
            base = sum(len(chunk) for chunk in chunks[1:]) // 2
            if c == n - 1:
                for j in range(FIXED, 2 * slots):
                    for t in range(3):
                        spare_ref[j - FIXED, base + t] = jnp.where(
                            core == 0, mine[inner][state["near"][j], t], mine[c][state["near"][j], t]
                        )
            return remote(gathered[c], arrived[c].at[core], x_s.at[c], x_r.at[c], partner)
        half = len(chunks[c]) // 2
        start = core * half
        for j in range(FIXED):
            for t in range(half):
                gathered[c][j, t] = mine[c][state["near"][j], start + t]
        base = sum(len(chunk) for chunk in chunks[1:c]) // 2
        for j in range(FIXED, 2 * slots):
            for t in range(half):
                spare_ref[j - FIXED, base + t] = mine[c][state["near"][j], start + t]
        return remote(gathered[c], arrived[c].at[core], x_s.at[c], x_r.at[c], partner)

    ready = [set(), set()]

    def compute(c):
        one = sorted({x + d for x in chunks[c] for d in range(-2, 3)} - ready[0])
        two = sorted({x + d for x in chunks[c] for d in range(-1, 2)} - ready[1])
        ready[0].update(one)
        ready[1].update(two)
        for x in one:
            for p in range(slots):
                first(p, x)
        for x in two:
            for p in range(slots):
                second(p, x)
        for at, x in enumerate(chunks[c]):
            for p in range(slots):
                third(p, x, mine[c], at)

    first_side = jnp.where(lon == 0, 1, 0)
    sides = {inner: first_side, inner + 1: 1 - first_side}

    def compute_edge(c):
        side = sides[c]
        for t in range(3):
            for p in range(slots):
                first(p, side * (cols + 1) - 2 + t)
        for t in range(3):
            for p in range(slots):
                second(p, side * (cols - 1) - 1 + t)
        for t in range(3):
            for p in range(slots):
                third(p, side * (cols - 3) + t, mine[c], t)

    compute(0)
    ends = pl.ds(core * slots, slots)
    crossings = [
        remote(mine[0].at[0:slots], arrived[0].at[ends], x_s.at[0], x_r.at[0], partner)
    ]

    shares = [share(0)]
    relay(2)
    for x0 in outer:
        turn(raw_obs, obs_cm, 0, x0)
    compute(1)
    shares.append(share(1))
    for r in range(3, n_lon):
        relay(r)

    @pl.when(lon == n_lon - 1)
    def _():
        edge(True, True)

    @pl.when(lon == 0)
    def _():
        edge(False, True)

    for copy in sent_anc:
        copy.wait()
    near, sources, remotes, most = choose()
    k_own[0] = most
    state["near"], state["sources"], state["remotes"] = near, sources, remotes
    state["ens"] = [
        remote(k_own, k_all.at[k - 1], ens_s.at[k - 1], ens_r.at[k - 1], ens_at(k))
        for k in range(1, n_ens)
    ]
    shares[0].wait()
    crossings.append(pass_on(1, shares[1]))
    compute(2)
    shares.append(share(2))
    crossings.append(pass_on(2, shares[2]))
    for c in range(3, inner):
        compute(c)
        shares.append(share(c))
        if c > 3:
            crossings.append(pass_on(c - 1, shares[c - 1]))
    for c in (inner, inner + 1):
        @pl.when(sides[c] == 0)
        def _():
            edge(True, False).wait_recv()
            for p in range(slots):
                for t in range(3):
                    ext[p, t, :rows] = halo_in[0, p, t]

        @pl.when(sides[c] == 1)
        def _():
            edge(False, False).wait_recv()
            for p in range(slots):
                for t in range(3):
                    ext[p, cols + 3 + t, :rows] = halo_in[1, p, t]

        compute_edge(c)
        shares.append(share(c))
        if c == inner:
            crossings.append(pass_on(c - 1, shares[c - 1]))
        crossings.append(pass_on(c, shares[c]))
    edge(True, False).wait_send()
    edge(False, False).wait_send()

    sums = [jnp.sum(misfit[p], axis=0, keepdims=True) for p in range(slots)]
    sums = [s[:, :128] + s[:, 128:] for s in sums]
    row = lax.broadcasted_iota(jnp.int32, (8, 128), 0)
    local = jnp.zeros((8, 128), f32)
    for p in range(slots):
        local = jnp.where(row == p, sums[p], local)
    lon_sum[...] = 4.0 * local
    sent = [
        remote(lon_sum, lon_parts.at[k - 1], lon_s.at[k - 1], lon_r.at[k - 1], lon_at(k))
        for k in range(1, n_lon)
    ]
    forwards = []

    def finish(c):
        forwards[c].wait()
        half = len(chunks[c]) // 2 if c < inner else 0
        for s in range(slots):
            src = state["sources"][s]
            near = jnp.minimum(src, 2 * slots - 1)
            far = jnp.clip(src - 2 * slots, 0, FIXED - 1)
            if c >= inner:
                for at in range(3):
                    out_ref[s, sides[c] * (cols - 3) + at] = jnp.where(
                        src < 2 * slots, mine[c][near, at], arrived[c][far, at]
                    )[:nvars]
                continue
            for at, x in enumerate(chunks[c]):
                if c == 0:
                    far_away = arrived[c][state["remotes"][s], at]
                else:
                    far_away = arrived[c][at // half, far, at % half]
                out_ref[s, x] = jnp.where(src < 2 * slots, mine[c][near, at], far_away)[:nvars]

    for c in range(n):
        crossings[c].wait()
        piece = arrived[c].at[ends if c == 0 else core]
        forwards.append(remote(piece, piece, fwd_s.at[c], fwd_r.at[c], sibling))
        if c == n - 3:
            for copy in sent:
                copy.wait()
            band = lon_sum[...]
            for k in range(1, n_lon):
                band = band + lon_parts[k - 1]
            dom_parts[0] = band
            sent = [
                remote(dom_parts.at[0], dom_parts.at[k], dom_s.at[k - 1], dom_r.at[k - 1], dom_at(k))
                for k in range(1, 4)
            ]
        if c > 0:
            finish(c - 1)
    for copy in sent:
        copy.wait()
    misfits = [jnp.broadcast_to(jnp.sum(dom_parts[k], axis=1, keepdims=True), (8, 128)) for k in range(4)]
    real = row < slots

    def over(values):
        total = values[0]
        for value in values[1:]:
            total = total + value
        return jnp.sum(jnp.where(real, total, 0.0), axis=0, keepdims=True)

    center = over(misfits) / (4 * slots)
    off = [m - center for m in misfits]
    spread = jnp.sqrt(over([d * d for d in off]) / (4 * slots) + 1.0)
    expos = [jnp.exp(-0.5 * temp_ref[0] * d / spread) for d in off]
    own = expos[0] / over(expos)
    lane = lax.broadcasted_iota(jnp.int32, (8, 128), 1)
    for s in range(slots):
        wts_ref[s] = jnp.sum(jnp.where((row == s) & (lane == 0), own, 0.0))
    finish(n - 1)

    most = k_own[0]
    for copy in state["ens"]:
        copy.wait()
    for k in range(1, n_ens):
        most = jnp.maximum(most, k_all[k - 1, 0])
    info_ref[0] = jnp.maximum(most - FIXED, 0)
    for s in range(slots):
        info_ref[1 + s] = state["sources"][s]


def main_call(particles, observed, precision, stations, ancestors, tempering, w_in, w_mid, w_out):
    slots, nvars, cols, lat = particles.shape
    hid = w_mid.shape[2]
    cin, rows = pad_to(nvars, 16), pad_to(nvars, 8)
    n_lon, n_ens = lax.axis_size("lon"), lax.axis_size("ens")
    chunks = column_chunks(cols)
    n = len(chunks) + 2
    bf16, f32 = jnp.bfloat16, jnp.float32
    vmem = pl.BlockSpec(memory_space=pltpu.VMEM)
    smem = pl.BlockSpec(memory_space=pltpu.SMEM)
    hbm = pl.BlockSpec(memory_space=pltpu.HBM)
    dma = pltpu.SemaphoreType.DMA
    scratch = [
        pltpu.VMEM((slots, nvars, cols, lat), bf16),
        pltpu.VMEM((nvars, cols, lat), bf16),
        pltpu.VMEM(precision.shape, f32),
        pltpu.VMEM(stations.shape, jnp.int32),
        pltpu.SMEM(ancestors.shape, jnp.int32),
        pltpu.SMEM(tempering.shape, f32),
        pltpu.VMEM(w_in.shape, bf16),
        pltpu.VMEM(w_mid.shape, bf16),
        pltpu.VMEM((3, 3) + w_out.shape[:1:-1], bf16),
        pltpu.VMEM((slots, cols + 6, cin, lat), bf16),
        pltpu.VMEM((cols, cin, lat), bf16),
        pltpu.VMEM((slots, cols + 4, hid, lat), bf16),
        pltpu.VMEM((slots, cols + 2, hid, lat), bf16),
        pltpu.VMEM((3 * hid, 3 * cin), bf16),
        pltpu.VMEM((3 * hid, 3 * hid), bf16),
        pltpu.VMEM((3 * cin, 3 * hid), bf16),
        pltpu.VMEM((cols, lat), f32),
        pltpu.VMEM((slots, 8, lat), f32),
        pltpu.SMEM((128,), jnp.int32),
        pltpu.SMEM((4, 128), jnp.int32),
        pltpu.SMEM((128,), jnp.int32),
        pltpu.SMEM((max(n_ens - 1, 1), 128), jnp.int32),
        pltpu.VMEM((8, 128), f32),
        pltpu.VMEM((max(n_lon - 1, 1), 8, 128), f32),
        pltpu.VMEM((4, 8, 128), f32),
        pltpu.VMEM((2, slots, 3, rows, lat), bf16),
        pltpu.VMEM((2, slots, 3, rows, lat), bf16),
    ]
    scratch += [pltpu.VMEM((2 * slots, len(c), rows, lat), bf16) for c in chunks]
    scratch += [pltpu.VMEM((2 * slots, 3, rows, lat), bf16)] * 2
    scratch += [pltpu.VMEM((FIXED, len(c) // 2, rows, lat), bf16) for c in chunks]
    scratch += [pltpu.VMEM((3, rows, lat), bf16)] * 2
    scratch += [pltpu.VMEM((2 * slots, len(chunks[0]), rows, lat), bf16)]
    scratch += [pltpu.VMEM((2, FIXED, len(c) // 2, rows, lat), bf16) for c in chunks[1:]]
    scratch += [pltpu.VMEM((2, 3, rows, lat), bf16)] * 2
    scratch += [dma((slots + 8,))] + [dma((3,))] * 2 + [dma((2,))] * 2 + [dma((n,))] * 6
    scratch += [dma((max(n_lon - 1, 1),))] * 2 + [dma((3,))] * 2 + [dma((max(n_ens - 1, 1),))] * 2
    scratch += [pltpu.SemaphoreType.REGULAR] * 2
    return pl.pallas_call(
        functools.partial(main_kernel, n_lon, n_ens, cin, hid, chunks),
        out_shape=(
            jax.ShapeDtypeStruct((slots, cols, nvars, lat), bf16),
            jax.ShapeDtypeStruct((2 * slots - FIXED, (cols - len(chunks[0])) // 2, rows, lat), bf16),
            jax.ShapeDtypeStruct((1 + slots,), jnp.int32),
            jax.ShapeDtypeStruct((slots,), f32),
        ),
        in_specs=[hbm] * 9,
        out_specs=(vmem, vmem, smem, smem),
        scratch_shapes=scratch,
        compiler_params=pltpu.CompilerParams(
            collective_id=0, has_side_effects=True, vmem_limit_bytes=62 << 20
        ),
        name="step",
    )(particles, observed, precision, stations, ancestors, tempering, w_in, w_mid, w_out.transpose(0, 1, 3, 2))


def more_kernel(extra, chunks, info_ref, out_in, spare_ref, out_ref, *rest):
    arrived, (x_s, x_r, fwd_s, fwd_r) = rest[: len(chunks)], rest[len(chunks) :]
    slots = out_in.shape[0]
    nvars = out_in.shape[2]
    dom = lax.axis_index("dom")
    core = lax.rem(dom, 2)
    sibling, partner = {"dom": dom + 1 - 2 * core}, {"dom": lax.rem(dom + 2, 4)}
    barrier = pltpu.get_barrier_semaphore()
    for peer in (sibling, partner):
        pl.semaphore_signal(barrier, inc=1, device_id=peer, device_id_type=MESH)
    pl.semaphore_wait(barrier, 2)
    cols = out_in.shape[1]
    first_side = jnp.where(lax.axis_index("lon") == 0, 1, 0)
    spans, at = [], 0
    for chunk in chunks[1:]:
        spans.append((at, len(chunk) // 2))
        at += len(chunk) // 2
    spans.append((at, 3))
    crossings = []
    for c, (lo, size) in enumerate(spans):
        crossings.append(remote(
            spare_ref.at[0:extra, pl.ds(lo, size)], arrived[c].at[core], x_s.at[c], x_r.at[c], partner
        ))
    sources = [info_ref[1 + s] for s in range(slots)]

    def settle(c):
        lo, size = spans[c]
        for s in range(slots):
            src = sources[s]
            far = jnp.clip(src - (2 * slots + FIXED), 0, extra - 1)
            for half in range(2):
                for t in range(size):
                    if c < len(chunks) - 1:
                        x = chunks[c + 1][half * size + t]
                    else:
                        side = first_side if half == 0 else 1 - first_side
                        x = side * (cols - 3) + t
                    out_ref[s, x] = jnp.where(
                        src < 2 * slots + FIXED, out_in[s, x], arrived[c][half, far, t][:nvars]
                    )

    for s in range(slots):
        for x in chunks[0]:
            out_ref[s, x] = out_in[s, x]
    forwards = []
    for c in range(len(spans)):
        crossings[c].wait()
        piece = arrived[c].at[core]
        forwards.append(remote(piece, piece, fwd_s.at[c], fwd_r.at[c], sibling))
        if c > 0:
            forwards[c - 1].wait()
            settle(c - 1)
    forwards[-1].wait()
    settle(len(spans) - 1)


def more_call(extra, info, out, spare):
    slots, cols, nvars, lat = out.shape
    chunks = column_chunks(cols)
    vmem = pl.BlockSpec(memory_space=pltpu.VMEM)
    dma = pltpu.SemaphoreType.DMA
    return pl.pallas_call(
        functools.partial(more_kernel, extra, chunks),
        out_shape=jax.ShapeDtypeStruct(out.shape, out.dtype),
        in_specs=[pl.BlockSpec(memory_space=pltpu.SMEM), vmem, pl.BlockSpec(memory_space=pltpu.HBM)],
        out_specs=vmem,
        scratch_shapes=[
            pltpu.VMEM((2, extra, size) + spare.shape[2:], out.dtype)
            for size in [len(chunk) // 2 for chunk in chunks[1:]] + [3]
        ] + [dma((len(chunks),))] * 4,
        compiler_params=pltpu.CompilerParams(
            collective_id=extra, has_side_effects=True, vmem_limit_bytes=24 << 20
        ),
        name="more",
    )(info, out, spare)


def two_chips(*args):
    out, spare, info, weights = main_call(*args)
    slots = out.shape[0]
    branches = [lambda info, out, spare: out]
    for extra in range(1, 2 * slots - FIXED + 1):
        branches.append(functools.partial(more_call, extra))
    out = lax.switch(info[0], branches, info, out, spare)
    return (out.transpose(0, 2, 1, 3), weights)


def on_device(*args):
    if lax.axis_size("dom") == 4 and args[0].shape[2] >= 16:
        return two_chips(*args)
    return many_chips(*args)


def solution(mesh):
    return jax.shard_map(
        on_device,
        mesh=mesh,
        in_specs=(
            P(("ens", "dom"), None, "lon", None),
            P("ens", "lon", None),
            P(("ens", "lon"), None),
            P(("ens", "lon"), None),
            P(("ens", "dom")),
            P("ens"),
            P(),
            P(),
            P(),
        ),
        out_specs=(P(("ens", "dom"), None, "lon", None), P(("ens", "dom"))),
        check_vma=False,
    )
```
